512 devices in a mesh: site: 32 (over x, y, core), tensor: 16 (over z).
Axes of the slice: x: 4, y: 4, z: 16, core: 2. Of those that a mesh axis runs over, the one named last changes fastest.
Arguments:
- mps: bfloat16 [32, 32, 4, 128, 128], P('site', 'tensor'), may hold values from -0.5 to 0.5
- mpo: bfloat16 [4, 10, 10, 4, 4], replicated, may hold values from -1 to 1
- mpo_mask: int32 [4, 10, 10], replicated, may hold values 0 or 1
- sector_size: int32 [32, 32], P('site', 'tensor'), may hold values from 16 to 128, as said below
- pair_live: int32 [32, 32, 3], P('site', 'tensor'), may hold values 0 or 1
Outputs:
- environment: bfloat16 [32, 32, 10, 128, 128], P('site', 'tensor')
The draws below stay inside these ranges and needn't reach their ends.
Inputs may be any that keep to these rules, and one draw needn't show every extreme that they name: `sector_size`: the last sector of every bond is kept at its full 128 states; sizes grow with the sector index on average.
All inputs are finite; a program needn't handle non-finite values. No bound on the sum of `pair_live` on one device may be relied on, other than what follows from the above.
Results may differ from the reference program's by a relative error of at most 0.014.
Values may be sent and summed in bfloat16 or wider, within the bound.
A program may use at most 64 MiB of HBM per device.

```python
import jax
import jax.numpy as jnp
from jax import lax

DS = 128
DW = 10
PHYS = 4
SITES = 4
SECTORS = 32
STATES = 8
CHAIN = 32


def draw_sector_size(key, part):
    sector_ids = jnp.arange(SECTORS, dtype=jnp.int32)
    lowest = DS // 8 + DS * 3 // 8 * sector_ids // max(SECTORS - 1, 1)
    raw = jax.random.randint(key, (CHAIN, SECTORS), 0, 1 << 20, dtype=jnp.int32)
    sizes = lowest[None, :] + raw % (lowest[None, :] + 1)
    sizes = jnp.where(sector_ids[None, :] == SECTORS - 1, DS, sizes)
    return sizes.astype(jnp.int32)


def with_ends(values, rng, smallest, largest):
    shape = values.shape
    index_at = [jax.random.randint(jax.random.fold_in(rng, axis), (), 0, shape[axis]) for axis in range(len(shape))]
    values = values.at[tuple(index_at)].set(smallest)
    longest = shape.index(max(shape))
    index_at[longest] = (index_at[longest] + 1) % shape[longest]
    return values.at[tuple(index_at)].set(largest)


def steps_of(own_key, shape, split, low, largest):
    gain = 1.0
    for position, shards_of in split:
        steps = jax.random.uniform(jax.random.fold_in(jax.random.fold_in(own_key, 6), position), (shards_of,), jnp.float32, low / len(split), largest / len(split))
        gain = gain * jnp.repeat(jnp.exp(steps), shape[position] // shards_of).reshape((-1,) + (1,) * (len(shape) - 1 - position))
    return gain


def gaussian(stream_key, shape, width, bound, pieces=(), held_as=jnp.bfloat16):
    factor_of = steps_of(stream_key, shape, pieces, -0.22, 0.18) if pieces else 1.0
    result = jax.random.normal(stream_key, shape, jnp.float32) * width * factor_of
    return jnp.minimum(jnp.maximum(result, -bound), bound).astype(held_as)


def setup_inputs(seed: int = 0) -> dict:
    key_of = jax.random.split(jax.random.key(seed), 6)
    return {
        "mps": gaussian(key_of[0], (CHAIN, SECTORS, PHYS, DS, DS), DS ** -0.5, 0.5, ((0, 32), (1, 16))),
        "mpo": gaussian(key_of[1], (SITES, DW, DW, PHYS, PHYS), (4 * DW) ** -0.5, 1.0),
        "mpo_mask": with_ends((jax.random.randint(key_of[2], (SITES, DW, DW), 0, 4) < 3).astype(jnp.int32), jax.random.fold_in(key_of[2], 1), 0, 1),
        "sector_size": draw_sector_size(jax.random.fold_in(key_of[5], 71), 0),
        "pair_live": with_ends((jax.random.randint(key_of[4], (CHAIN, SECTORS, 3), 0, 5) < 4).astype(jnp.int32), jax.random.fold_in(key_of[4], 1), 0, 1),
    }


epsilon = 1e-06

def rounded(value):
    return lax.optimization_barrier(value.astype(jnp.bfloat16)).astype(jnp.float32)

def reference(mps, mpo, mpo_mask, sector_size, pair_live):
    charge = jnp.array([0, 1, 1, 2], jnp.int32)
    same = charge[:, None] == charge[None, :]
    weights = jnp.where((mpo_mask[:, :, :, None, None] > 0) & same[None, None, None, :, :], mpo, jnp.zeros_like(mpo)).astype(jnp.float32)
    sector_ids = jnp.arange(SECTORS, dtype=jnp.int32)
    live_state = pair_live[:, :, charge] > 0
    inside = sector_ids[:, None] + charge[None, :] < SECTORS
    rows_kept = jnp.arange(DS, dtype=jnp.int32)[None, None, :] < sector_size[:, :, None]
    keep = (live_state & inside[None, :, :])[:, :, :, None, None] & rows_kept[:, :, None, :, None]
    masked = jnp.where(keep, mps, jnp.zeros_like(mps)).astype(jnp.float32)
    channel = jnp.arange(DW, dtype=jnp.int32)
    boundary = ((channel[:, None, None] == DW - 1) & (jnp.eye(DS, dtype=jnp.float32)[None] > 0)).astype(jnp.float32)
    entries = float(SECTORS * DW * DS * DS)

    def advance(padded, blocks, site_weights):

        def sector(index):
            here = lax.dynamic_index_in_dim(padded, index, 0, keepdims=False)
            above = lax.dynamic_index_in_dim(padded, index + 1, 0, keepdims=False)
            beyond = lax.dynamic_index_in_dim(padded, index + 2, 0, keepdims=False)
            local = lax.dynamic_index_in_dim(blocks, index, 0, keepdims=False)
            part_low = jnp.einsum('ab,vbc->avc', local[0], here)
            part_mid = jnp.einsum('sab,vbc->savc', local[1:3], above)
            part_top = jnp.einsum('ab,vbc->avc', local[3], beyond)
            inner = rounded(jnp.concatenate([part_low[None], part_mid, part_top[None]], 0))
            mixed = rounded(jnp.einsum('xavb,wvxy->ywab', inner, site_weights))
            return jnp.einsum('ywab,ycb->wac', mixed, local)
        block = lax.map(sector, jnp.arange(SECTORS, dtype=jnp.int32))
        square = jnp.sum(block * block) / entries
        return (block * lax.rsqrt(square + epsilon)).astype(jnp.bfloat16)
    results = [None] * CHAIN
    for group in range(STATES):
        padded = jnp.broadcast_to(boundary, (SECTORS + 2, DW, DS, DS))
        for place in reversed(range(SITES)):
            entry = (group * SITES + place - 1) % CHAIN
            fresh = advance(padded, masked[entry], weights[place])
            results[entry] = fresh
            padded = jnp.concatenate([fresh.astype(jnp.float32), jnp.zeros((2, DW, DS, DS), jnp.float32)], 0)
    return jnp.stack(results, 0)
```

```python
import functools

import jax
import jax.numpy as jnp
from jax import lax
from jax.experimental import pallas as pl
from jax.experimental.pallas import tpu as pltpu
from jax.sharding import PartitionSpec as P

SITES = 4
MESH = pl.DeviceIdType.MESH
EPSILON = 1e-06
HALF = 2.0**-12
F32 = jnp.float32
BF16 = jnp.bfloat16
REACH = 4


def nt(a, b):
    return lax.dot_general(a, b, (((1,), (1,)), ((), ())), preferred_element_type=F32)


def nn(a, b):
    return lax.dot_general(a, b, (((1,), (0,)), ((), ())), preferred_element_type=F32)


def spread(small, channels, first, count):
    rows = count * channels * 8
    ids = lax.broadcasted_iota(jnp.int32, (rows, small.shape[0]), 0) // 8 + first * channels
    pick = (ids == lax.broadcasted_iota(jnp.int32, (rows, small.shape[0]), 1)).astype(BF16)
    wide = nt(nn(pick, small).astype(BF16), pick)
    same = (
        lax.broadcasted_iota(jnp.int32, (rows, rows), 0) % 8
        == lax.broadcasted_iota(jnp.int32, (rows, rows), 1) % 8
    )
    return jnp.where(same, wide, 0.0).astype(BF16)


def kernel(
    m_ref, first_ref, mix_ref, out_ref,
    m_all, r_all, mix_low, mix_mid, mix_top, mixed, squares, mine, heard, final,
    send_sem, recv_sem, local_sem, done_sem, result_send, result_recv, sum_send, sum_recv,
    near_sem, middle_sem, far_sem,
):
    site, place = lax.axis_index("site"), lax.axis_index("tensor")
    sites, places = lax.axis_size("site"), lax.axis_size("tensor")
    role = site % SITES
    hub = jnp.where(role == 3, (site + 1) % sites, site - role)
    channels, width = r_all.shape[2], r_all.shape[3]
    held = m_ref.shape[0]

    def at(step):
        return lax.rem(place + step + places, places)

    barrier = pltpu.get_barrier_semaphore()

    def greet(site_to, place_to):
        pl.semaphore_signal(barrier, inc=1, device_id=(site_to, place_to), device_id_type=MESH)

    near = [s for k in range(1, REACH) for s in (k, -k)]

    @pl.when(role == 0)
    def _():
        for k in range(REACH):
            greet(hub + 2, at(k))
        for k in range(REACH - 1):
            greet(hub + 1, at(k))
        for s in near:
            greet(hub, at(s))
        greet((hub + sites - 1) % sites, place)
        pl.semaphore_wait(barrier, 2 * REACH + len(near))

    @pl.when(role == 1)
    def _():
        for k in range(REACH - 1):
            greet(hub, at(-k))
        pl.semaphore_wait(barrier, REACH - 1)

    @pl.when(role == 2)
    def _():
        for k in range(REACH):
            greet(hub, at(-k))
        pl.semaphore_wait(barrier, REACH)

    @pl.when(role == 3)
    def _():
        greet(hub, place)
        pl.semaphore_wait(barrier, 1)

    def blocks(turn, k):
        return pltpu.make_async_remote_copy(
            src_ref=m_ref,
            dst_ref=m_all.at[turn, pl.ds(held * k, held)],
            send_sem=send_sem.at[k],
            recv_sem=recv_sem.at[turn, k],
            device_id=(hub, at(-k)),
            device_id_type=MESH,
        )

    def own(turn):
        return pltpu.make_async_copy(m_ref, m_all.at[turn, pl.ds(0, held)], local_sem)

    def start(sector):
        low = m_all[0, sector, 0]
        mid = m_all[0, sector, 1:3].reshape(2 * width, width)
        top = m_all[0, sector, 3]
        step = 32
        total = jnp.zeros((8, width), F32)
        for row in range(0, width, step):
            g0 = nt(low[row : row + step], low)
            g1 = nt(mid[row : row + step], mid)
            g2 = nt(mid[width + row : width + row + step], mid)
            g3 = nt(top[row : row + step], top)
            parts = (g0, g1[:, :width], g1[:, width:], g2[:, :width], g2[:, width:], g3)
            for w in range(channels):
                block = parts[0] * first_ref[w, 0]
                for i in range(1, 6):
                    block = block + parts[i] * first_ref[w, i]
                r_all[0, sector, w, row : row + step, :] = block.astype(BF16)
                small = block * HALF
                total = total + jnp.sum((small * small).reshape(step // 8, 8, width), axis=0)
        slot = (sector >= held).astype(jnp.int32)
        squares[slot, 0] += total

    def advance(turn, sector):
        prev = turn - 1
        low = m_all[turn, sector, 0]
        mid = m_all[turn, sector, 1:3].reshape(2 * width, width)
        top = m_all[turn, sector, 3]
        step = 32

        def pairs(x):
            y = x.reshape(channels, step // 8, 8, width)
            cut = lambda i: y[:, i].reshape(channels * 8, width)
            return [
                jnp.concatenate([cut(2 * j), cut(2 * j + 1)], axis=1).astype(BF16)
                for j in range(step // 16)
            ]

        k_low, k_mid, k_top = mix_low[prev], mix_mid[prev], mix_top[prev]
        for row in range(0, width, step):
            def rows_of(q):
                return r_all[prev, q, :, row : row + step, :].reshape(channels * step, width)

            x0 = pairs(nt(rows_of(sector), low))
            x12 = nt(rows_of(sector + 1), mid)
            x1, x2 = pairs(x12[:, :width]), pairs(x12[:, width:])
            x3 = pairs(nt(rows_of(sector + 2), top))
            for j in range(step // 16):
                y0 = nn(k_low, x0[j])
                y12 = nn(k_mid, jnp.concatenate([x1[j], x2[j]], axis=0))
                y3 = nn(k_top, x3[j])
                for s, y in ((0, y0), (1, y12[: channels * 8]), (2, y12[channels * 8 :]), (3, y3)):
                    z = y.reshape(channels, 8, 2 * width)
                    at_row = s * width + row + 16 * j
                    for w in range(channels):
                        both = jnp.concatenate([z[w, :, :width], z[w, :, width:]], axis=0)
                        lane = (w % 2) * width
                        mixed[w // 2, at_row : at_row + 16, lane : lane + width] = both.astype(BF16)
        wide = jnp.concatenate([low, mid[:width], mid[width:], top], axis=1)
        total = jnp.zeros((8, 2 * width), F32)
        for pair in range(channels // 2):
            block = nn(wide, mixed[pair])
            r_all[turn, sector, 2 * pair] = block[:, :width].astype(BF16)
            r_all[turn, sector, 2 * pair + 1] = block[:, width:].astype(BF16)
            small = block * HALF
            total = total + jnp.sum((small * small).reshape(width // 8, 8, 2 * width), axis=0)
        slot = (sector >= held).astype(jnp.int32)
        squares[slot, turn] += total[:, :width] + total[:, width:]

    def result(turn, sector, count, site_to):
        part = r_all.at[turn, pl.ds(sector, count)]
        return pltpu.make_async_remote_copy(
            src_ref=part, dst_ref=part,
            send_sem=result_send.at[turn, sector], recv_sem=result_recv.at[turn, sector],
            device_id=(site_to, place), device_id_type=MESH,
        )

    last_site = (hub + sites - 1) % sites

    @pl.when(role == 1)
    def _():
        for k in range(REACH - 1):
            blocks(1, k).start()

    @pl.when(role == 2)
    def _():
        for k in range(REACH):
            blocks(0, k).start()
        own(0).start()
        own(0).wait()

        @pl.loop(0, held)
        def _(j):
            start(j)

    @pl.when(role == 3)
    def _():
        blocks(3, 0).start()

    def tell(sem, step):
        pl.semaphore_signal(sem, inc=1, device_id=(hub, at(step)), device_id_type=MESH)

    def sum_copy(kind, step, site_to):
        return pltpu.make_async_remote_copy(
            src_ref=mine, dst_ref=heard.at[place],
            send_sem=sum_send.at[kind, step], recv_sem=sum_recv,
            device_id=(site_to, at(step)), device_id_type=MESH,
        )

    @pl.when(role == 0)
    def _():
        own(2).start()
        blocks(2, 1).start()
        for s in near:
            tell(near_sem, s)
        squares[...] = jnp.zeros_like(squares)
        for i in range(SITES - 1):
            small = mix_ref[i]
            mix_low[i] = spread(small, channels, 0, 1)
            mix_mid[i] = spread(small, channels, 1, 2)
            mix_top[i] = spread(small, channels, 3, 1)
        own(2).wait()
        pl.semaphore_wait(near_sem, len(near))
        for s in near:
            tell(middle_sem, s)

        @pl.loop(0, REACH)
        def _(k):
            blocks(0, k).wait_recv()

            @pl.loop(0, held)
            def _(j):
                start(held * k + j)

            @pl.loop(1, k + 1)
            def _(t):
                @pl.when(t == 1)
                def _():
                    blocks(1, k - 1).wait_recv()

                @pl.when((t == 2) & (k == 3))
                def _():
                    blocks(2, 1).wait_recv()

                @pl.when(t == 3)
                def _():
                    blocks(3, 0).wait_recv()

                @pl.loop(0, held)
                def _(j):
                    advance(t, held * (k - t) + j)

                    @pl.when(t == 3)
                    def _():
                        result(3, j, 1, last_site).start()

            @pl.when(k == 0)
            def _():
                pl.semaphore_wait(middle_sem, len(near))
                for s in near:
                    tell(far_sem, s)

            @pl.when(k == 1)
            def _():
                result(1, 0, held, hub + 1).start()

        lane = lax.broadcasted_iota(jnp.int32, (1, width), 1)
        row = jnp.zeros((1, width), F32)
        for t in range(SITES):
            row = row + jnp.where(lane == t, jnp.sum(squares[0, t]), 0.0)
        mine[...] = row
        heard[place] = row
        pl.semaphore_wait(far_sem, len(near))

        @pl.loop(0, places)
        def _(step):
            sum_copy(3, step, last_site).start()

        @pl.loop(0, places)
        def _(step):
            sum_copy(1, step, hub + 1).start()
            sum_copy(2, step, hub + 2).start()

        @pl.loop(1, places)
        def _(step):
            sum_copy(0, step, hub).start()

    @pl.when(role == 3)
    def _():
        for j in range(held):
            result(3, j, 1, last_site).wait_recv()

    @pl.when(role == 1)
    def _():
        result(1, 0, held, hub + 1).wait_recv()

    def heard_all(count):
        part = heard.at[pl.ds(0, count)]
        return pltpu.make_async_remote_copy(
            src_ref=part, dst_ref=part, send_sem=sum_send.at[0, 0], recv_sem=sum_recv,
            device_id=(site, at(1)), device_id_type=MESH,
        )

    @pl.when(role == 0)
    def _():
        heard_all(places - 1).wait_recv()

    @pl.when(role != 0)
    def _():
        heard_all(places).wait_recv()

    turn = jnp.where(role == 3, 3, 2 - role)
    sums = jnp.sum(heard[...].reshape(places, width), axis=0, keepdims=True)
    entries = float(places * held * channels * width * width)
    unit = jnp.ones((1, 1), F32)
    chosen = unit
    for t in range(SITES):
        square = sums[:, t : t + 1] * (1.0 / (HALF * HALF * entries)) * unit * unit
        unit = unit * lax.rsqrt(square + EPSILON)
        chosen = jnp.where(turn == t, unit, chosen)

    def put(w):
        return pltpu.make_async_copy(final.at[:, w], out_ref.at[:, w], done_sem.at[w])

    for w in range(channels):
        final[:, w] = (r_all[turn, pl.ds(0, held), w].astype(F32) * chosen[None]).astype(BF16)
        put(w).start()
    for w in range(channels):
        put(w).wait()

    @pl.when(role == 0)
    def _():
        blocks(2, 1).wait_send()
        result(1, 0, held, hub + 1).wait_send()
        for j in range(held):
            result(3, j, 1, last_site).wait_send()

        @pl.loop(0, places)
        def _(step):
            for kind in (1, 2, 3):
                sum_copy(kind, step, hub).wait_send()

        @pl.loop(1, places)
        def _(step):
            sum_copy(0, step, hub).wait_send()

    @pl.when(role == 1)
    def _():
        for k in range(REACH - 1):
            blocks(1, k).wait_send()

    @pl.when(role == 2)
    def _():
        for k in range(REACH):
            blocks(0, k).wait_send()

    @pl.when(role == 3)
    def _():
        blocks(3, 0).wait_send()


def on_device(mps, mpo, mpo_mask, sector_size, pair_live):
    tensor_count = lax.axis_size("tensor")
    tensor_place = lax.axis_index("tensor")
    blocks_in = mps[0]
    held, phys = blocks_in.shape[:2]
    width = blocks_in.shape[-1]
    channels = mpo.shape[1]
    charge = jnp.array([0, 1, 1, 2], jnp.int32)
    live = pair_live[0]
    live_state = jnp.stack([live[:, 0], live[:, 1], live[:, 1], live[:, 2]], 1) > 0
    sector_ids = tensor_place * held + jnp.arange(held, dtype=jnp.int32)
    inside = sector_ids[:, None] + charge[None, :] < tensor_count * held
    rows_kept = jnp.arange(width, dtype=jnp.int32)[None, :] < sector_size[0][:, None]
    keep = (live_state & inside)[:, :, None, None] & rows_kept[:, None, :, None]
    masked = jnp.where(keep, blocks_in, jnp.zeros_like(blocks_in))
    same = charge[:, None] == charge[None, :]
    weights = jnp.where(
        (mpo_mask[:, :, :, None, None] > 0) & same[None, None, None], mpo, jnp.zeros_like(mpo)
    )
    edge = weights[SITES - 1, :, channels - 1].astype(F32).reshape(channels, phys * phys)
    first = jnp.stack([edge[:, i] for i in (0, 5, 6, 9, 10, 15)], 1)
    mix = jnp.transpose(weights[SITES - 2 :: -1], (0, 3, 1, 4, 2))
    mix = mix.reshape(SITES - 1, phys * channels, phys * channels)
    vmem = pltpu.VMEM
    dma = pltpu.SemaphoreType.DMA
    environment = pl.pallas_call(
        kernel,
        out_shape=jax.ShapeDtypeStruct((held, channels, width, width), BF16),
        in_specs=[
            pl.BlockSpec(memory_space=pl.ANY),
            pl.BlockSpec(memory_space=pltpu.SMEM),
            pl.BlockSpec(memory_space=pltpu.VMEM),
        ],
        out_specs=pl.BlockSpec(memory_space=pl.ANY),
        scratch_shapes=[
            vmem((SITES, held * REACH, phys, width, width), BF16),
            vmem((SITES, held * REACH, channels, width, width), BF16),
            vmem((SITES - 1, channels * 8, channels * 8), BF16),
            vmem((SITES - 1, channels * 16, channels * 16), BF16),
            vmem((SITES - 1, channels * 8, channels * 8), BF16),
            vmem((channels // 2, phys * width, 2 * width), BF16),
            vmem((2, SITES, 8, width), F32),
            vmem((1, width), F32),
            vmem((tensor_count, 1, width), F32),
            vmem((held, channels, width, width), BF16),
            dma((REACH,)),
            dma((SITES, REACH)),
            dma,
            dma((channels,)),
            dma((SITES, held)),
            dma((SITES, held)),
            dma((SITES, tensor_count)),
            dma,
            pltpu.SemaphoreType.REGULAR,
            pltpu.SemaphoreType.REGULAR,
            pltpu.SemaphoreType.REGULAR,
        ],
        compiler_params=pltpu.CompilerParams(
            collective_id=0, has_side_effects=True, vmem_limit_bytes=60 * 1024 * 1024
        ),
    )(masked, first, mix)
    return environment[None]


def solution(mesh):
    in_specs = (
        P("site", "tensor", None, None, None),
        P(),
        P(),
        P("site", "tensor"),
        P("site", "tensor", None),
    )
    out_specs = P("site", "tensor", None, None, None)
    return jax.shard_map(
        on_device, mesh=mesh, in_specs=in_specs, out_specs=out_specs, check_vma=False
    )
```

```python
import jax
import jax.numpy as jnp
from jax import lax
from jax.experimental import pallas as pl
from jax.experimental.pallas import tpu as pltpu
from jax.sharding import PartitionSpec as P

SITES = 4
PHYS = 4
CHARGE = (0, 1, 1, 2)
PAIRS = (0, 5, 6, 9, 10, 15)
ROUNDS = (1, 2, 4, 1)
MESH = pl.DeviceIdType.MESH
EPSILON = 1e-06
SMALL = 2.0**-12
F32 = jnp.float32
BF16 = jnp.bfloat16
REACH = 4


def nt(a, b):
    return lax.dot_general(a, b, (((1,), (1,)), ((), ())), preferred_element_type=F32)


def nn(a, b):
    return lax.dot_general(a, b, (((1,), (0,)), ((), ())), preferred_element_type=F32)


def ids(rows, columns, axis):
    return lax.broadcasted_iota(jnp.int32, (rows, columns), axis)


def table_of(p, mpo_ref, mask_ref, table):
    channels = mask_ref.shape[0]
    table[...] = jnp.zeros_like(table)
    for w in range(channels):
        keep = mask_ref[w, p : p + 1, :] > 0
        for s in range(PHYS):
            tile = jnp.where(keep, mpo_ref[p, w, s].astype(F32), 0.0)
            at = (w * PHYS + s) * PHYS
            table[at : at + PHYS, :channels] = tile
    return table[...].astype(BF16)


def one_hot(condition):
    return jnp.where(condition, 1.0, 0.0).astype(BF16)


def spread(table, channels, first, count):
    one = channels * 8
    size, depth = count * one, table.shape[0]

    def split(x):
        state = jnp.where(x >= one, 1, 0)
        return state + first, (x - state * one) // 8

    _, channel_of_column = split(ids(table.shape[1], size, 1))
    wide = nn(table, one_hot(ids(table.shape[1], size, 0) == channel_of_column))
    state_of_column, _ = split(ids(depth, size, 1))
    wide = jnp.where(ids(depth, size, 0) % PHYS == state_of_column, wide, 0.0).astype(BF16)
    state_of_row, channel_of_row = split(ids(size, depth, 0))
    entry = ids(size, depth, 1)
    pick = one_hot(entry // PHYS == channel_of_row * PHYS + state_of_row)
    full = nn(pick, wide)
    return jnp.where(ids(size, size, 0) % 8 == ids(size, size, 1) % 8, full, 0.0).astype(BF16)


def edge_of(table, channels, coef):
    depth, lanes = table.shape
    last = nn(table, one_hot(ids(lanes, lanes, 0) == channels - 1)).astype(BF16)
    rows = channels * 8
    for i, code in enumerate(PAIRS):
        pick = one_hot(ids(rows, depth, 1) == ids(rows, depth, 0) // 8 * PHYS * PHYS + code)
        coef[i] = nn(pick, last).reshape(channels, 8, lanes)


def kernel(
    m_ref, mpo_ref, mask_ref, size_ref, live_ref, out_ref, scale_ref,
    raw, ring, m_all, r_all, mix_low, mix_mid, mix_top, coef, table, mixed, squares, mine, heard,
    raw_sem, ring_send, ring_recv, feed_send, feed_recv, pass_send, swap_send, swap_recv,
    last_send, last_recv, sum_send, sum_recv, round_sem,
):
    site, place = lax.axis_index("site"), lax.axis_index("tensor")
    sites, places = lax.axis_size("site"), lax.axis_size("tensor")
    role = site % SITES
    hub = jnp.where(role == 3, (site + 1) % sites, site - role)
    channels, width = r_all.shape[3], r_all.shape[4]
    held = m_ref.shape[0]
    far = hub + 2
    end = (hub + sites - 1) % sites
    parity = jnp.where(role == 1, 1, 0)
    partner = hub + 1 - parity
    works = role < 2

    def at(step):
        return lax.rem(place + step + places, places)

    load = pltpu.make_async_copy(m_ref, raw, raw_sem)
    load.start()
    barrier = pltpu.get_barrier_semaphore()

    def greet(*targets):
        for site_to, place_to in targets:
            pl.semaphore_signal(barrier, inc=1, device_id=(site_to, place_to), device_id_type=MESH)

    @pl.when(works)
    def _():
        greet((far, place), (end, place), (partner, place), (site, at(1)), (site, at(-1)))

    @pl.when(role == 2)
    def _():
        greet((hub, place), (hub + 1, place), (site, at(1)), (site, at(-1)))

    @pl.when(role == 3)
    def _():
        greet((hub, place), (hub + 1, place))

    load.wait()
    for i in range(held):
        sector = place * held + i
        for s in range(PHYS):
            charge = CHARGE[s]
            live = (live_ref[0, i, charge] > 0) & (sector + charge < places * held)
            bound = jnp.where(live, size_ref[0, i], 0)
            block = jnp.where(ids(width, width, 0) < bound, raw[i, s].astype(F32), 0.0)
            ring[0, i, s] = block.astype(BF16)

    def remote(src, dst, send, recv, site_to, place_to):
        return pltpu.make_async_remote_copy(
            src_ref=src, dst_ref=dst, send_sem=send, recv_sem=recv,
            device_id=(site_to, place_to), device_id_type=MESH,
        )

    def ring_copy(k, i):
        return remote(
            ring.at[k, i], ring.at[k + 1, i], ring_send.at[k, i], ring_recv.at[k + 1, i],
            site, at(-1),
        )

    def ring_wait(k, i):
        remote(
            ring.at[k, i], ring.at[k, i], ring_send.at[0, 0], ring_recv.at[k, i], site, at(-1)
        ).wait_recv()

    def feed(turn, k, i, source, send):
        return remote(
            source, m_all.at[turn, k], send, feed_recv.at[turn, k], hub + i, place
        )

    def feed_wait(turn, k):
        part = m_all.at[turn, k]
        remote(
            part, part, pass_send.at[0, 0], feed_recv.at[turn, k], partner, place
        ).wait_recv()

    def pass_on(turn, k):
        return remote(
            m_all.at[turn, k], m_all.at[turn, k + 1], pass_send.at[turn, k],
            feed_recv.at[turn, k + 1], site, at(-1),
        )

    def pass_first(turn):
        return remote(
            ring.at[0, parity], m_all.at[turn, 1], pass_send.at[turn, 0],
            feed_recv.at[turn, 1], site, at(-1),
        )

    def start(blocks, target, slot):
        low = blocks[0]
        mid = blocks[1:3].reshape(2 * width, width)
        top = blocks[3]
        step = 32
        total = jnp.zeros((8, width), F32)
        for row in range(0, width, step):
            g0 = nt(low[row : row + step], low)
            g1 = nt(mid[row : row + step], mid)
            g2 = nt(mid[width + row : width + row + step], mid)
            g3 = nt(top[row : row + step], top)
            parts = (g0, g1[:, :width], g1[:, width:], g2[:, :width], g2[:, width:], g3)
            parts = [x.reshape(step // 8, 8, width) for x in parts]
            for w in range(channels):
                block = parts[0] * coef[0, w][None]
                for i in range(1, len(PAIRS)):
                    block = block + parts[i] * coef[i, w][None]
                target[w, row : row + step, :] = block.reshape(step, width).astype(BF16)
                small = block * SMALL
                total = total + jnp.sum(small * small, axis=0)
        squares[slot, 0] += total

    def last_copy(i, pair):
        part = r_all.at[3, i, 0, pl.ds(2 * pair, 2)]
        return remote(part, part, last_send.at[pair], last_recv.at[i, pair], end, place)

    def advance(turn, j):
        prev = turn - 1
        low = m_all[turn, j, 0]
        mid = m_all[turn, j, 1:3].reshape(2 * width, width)
        top = m_all[turn, j, 3]
        step = 32

        def pairs(x):
            y = x.reshape(channels, step // 8, 8, width)
            cut = lambda i: y[:, i].reshape(channels * 8, width)
            return [
                jnp.concatenate([cut(2 * j), cut(2 * j + 1)], axis=1).astype(BF16)
                for j in range(step // 16)
            ]

        k_low, k_mid, k_top = mix_low[prev], mix_mid[prev], mix_top[prev]
        for row in range(0, width, step):
            def rows_of(which, slot):
                rows = r_all[prev, which, slot, :, row : row + step, :]
                return rows.reshape(channels * step, width)

            x0 = pairs(nt(rows_of(parity, j), low))
            x12 = nt(rows_of(1 - parity, j + parity), mid)
            x1, x2 = pairs(x12[:, :width]), pairs(x12[:, width:])
            x3 = pairs(nt(rows_of(parity, j + 1), top))
            for i in range(step // 16):
                y0 = nn(k_low, x0[i])
                y12 = nn(k_mid, jnp.concatenate([x1[i], x2[i]], axis=0))
                y3 = nn(k_top, x3[i])
                for s, y in ((0, y0), (1, y12[: channels * 8]), (2, y12[channels * 8 :]), (3, y3)):
                    z = y.reshape(channels, 8, 2 * width)
                    at_row = s * width + row + 16 * i
                    for w in range(channels):
                        both = jnp.concatenate([z[w, :, :width], z[w, :, width:]], axis=0)
                        lane = (w % 2) * width
                        mixed[w // 2, at_row : at_row + 16, lane : lane + width] = both.astype(BF16)
        wide = jnp.concatenate([low, mid[:width], mid[width:], top], axis=1)
        total = jnp.zeros((8, 2 * width), F32)
        for pair in range(channels // 2):
            block = nn(wide, mixed[pair])
            r_all[turn, parity, j, 2 * pair] = block[:, :width].astype(BF16)
            r_all[turn, parity, j, 2 * pair + 1] = block[:, width:].astype(BF16)
            small = block * SMALL
            total = total + jnp.sum((small * small).reshape(width // 8, 8, 2 * width), axis=0)
        slot = (j >= 1).astype(jnp.int32)
        squares[slot, turn] += total[:, :width] + total[:, width:]

    def swap(turn, j):
        part = r_all.at[turn, parity, j]
        return remote(part, part, swap_send.at[turn, j], swap_recv.at[turn, j], partner, place)

    def swap_wait(turn, j):
        part = r_all.at[turn, 1 - parity, j]
        remote(
            part, part, swap_send.at[turn, j], swap_recv.at[turn, j], partner, place
        ).wait_recv()

    def swaps(turn, j):
        even = (parity == 0) & ((j >= 1) | (turn == 1))
        odd = (parity == 1) & (j <= 2 - turn)
        return (turn < 3) & (even | odd)

    def tell(i):
        for step in (ROUNDS[i], -ROUNDS[i]):
            pl.semaphore_signal(
                round_sem.at[i], inc=1, device_id=(site, at(step)), device_id_type=MESH
            )

    def told(i):
        pl.semaphore_wait(round_sem.at[i], 2)

    targets = (end, hub, hub + 1, far)

    def sum_copy(kind, step):
        return remote(
            mine, heard.at[parity * places + place], sum_send.at[kind, step], sum_recv,
            targets[kind], at(step),
        )

    def sum_self(kind, step):
        return (step == 0) & (kind == parity + 1)

    @pl.when(role == 2)
    def _():
        pl.semaphore_wait(barrier, 4)

        @pl.loop(0, REACH)
        def _(k):
            for i in range(held):
                @pl.when(k > 0)
                def _():
                    ring_wait(k, i)

                @pl.when(k < REACH - 1)
                def _():
                    ring_copy(k, i).start()

                feed(0, k, i, ring.at[k, i], feed_send.at[k, i]).start()

        edge_of(table_of(SITES - 1, mpo_ref, mask_ref, table), channels, coef)
        squares[...] = jnp.zeros_like(squares)

        @pl.loop(0, held)
        def _(i):
            start(ring.at[0, i], r_all.at[0, i, 0], 1)

    @pl.when(role == 3)
    def _():
        pl.semaphore_wait(barrier, 2)
        for i in range(held):
            feed(3, 0, i, ring.at[0, i], feed_send.at[0, i]).start()

    @pl.when(works)
    def _():
        home = 2 - parity
        pl.semaphore_wait(barrier, 5)
        tell(0)
        feed(home, 0, 1 - parity, ring.at[0, 1 - parity], feed_send.at[0, 0]).start()
        pass_first(home).start()
        m_all[home, 0] = ring[0, parity]
        edge_of(table_of(SITES - 1, mpo_ref, mask_ref, table), channels, coef)
        squares[...] = jnp.zeros_like(squares)
        feed_wait(1 + parity, 0)
        pass_on(1 + parity, 0).start()
        told(0)
        tell(1)
        for turn in range(1, SITES):
            found = table_of(SITES - 1 - turn, mpo_ref, mask_ref, table)
            mix_low[turn - 1] = spread(found, channels, 0, 1)
            mix_mid[turn - 1] = spread(found, channels, 1, 2)
            mix_top[turn - 1] = spread(found, channels, 3, 1)
        feed_wait(1, 1)
        pass_on(1, 1).start()
        told(1)
        tell(2)

        @pl.loop(0, REACH)
        def _(k):
            feed_wait(0, k)
            start(m_all.at[0, k], r_all.at[0, parity, k], (k >= 1).astype(jnp.int32))

            @pl.when(swaps(0, k))
            def _():
                swap(0, k).start()

            @pl.loop(1, k + 1)
            def _(t):
                @pl.when(k == REACH - 1)
                def _():
                    feed_wait(t, k - t)

                swap_wait(t - 1, k - t + parity)
                advance(t, k - t)

                @pl.when(swaps(t, k - t))
                def _():
                    swap(t, k - t).start()

                @pl.when(t == 3)
                def _():
                    for pair in range(channels // 2):
                        last_copy(parity, pair).start()

            @pl.when(k == 1)
            def _():
                told(2)
                tell(3)

        lane = ids(1, width, 1)
        row = jnp.zeros((1, width), F32)
        for t in range(SITES):
            row = row + jnp.where(lane == t, jnp.sum(squares[0, t]), 0.0)
        mine[...] = row
        heard[parity * places + place] = row
        told(3)

        for kind in range(4):
            @pl.loop(0, places)
            def _(step):
                @pl.when(jnp.logical_not(sum_self(kind, step)))
                def _():
                    sum_copy(kind, step).start()

    def heard_all(count):
        part = heard.at[pl.ds(0, count)]
        remote(part, part, sum_send.at[0, 0], sum_recv, site, at(1)).wait_recv()

    @pl.when(role == 3)
    def _():
        for i in range(held):
            for pair in range(channels // 2):
                last_copy(i, pair).wait_recv()

    @pl.when(role == 1)
    def _():
        swap_wait(1, 0)

    @pl.when(works)
    def _():
        heard_all(2 * places - 1)

    @pl.when(role >= 2)
    def _():
        heard_all(2 * places)

    turn = jnp.where(role == 3, 3, 2 - role)
    sums = jnp.sum(heard[...].reshape(2 * places, width), axis=0, keepdims=True)
    entries = float(places * held * channels * width * width)
    unit = jnp.ones((1, 1), F32)
    chosen = unit
    for t in range(SITES):
        square = sums[:, t : t + 1] * (1.0 / (SMALL * SMALL * entries)) * unit * unit
        unit = unit * lax.rsqrt(square + EPSILON)
        chosen = jnp.where(turn == t, unit, chosen)
    scale_ref[...] = jnp.broadcast_to(chosen, scale_ref.shape)
    for i in range(held):
        out_ref[i] = r_all[turn, i, 0]

    @pl.when(works)
    def _():
        home = 2 - parity
        feed(home, 0, 1 - parity, ring.at[0, 1 - parity], feed_send.at[0, 0]).wait_send()
        for t, k in ((1, 0), (1, 1), (2, 0)):
            pass_on(t, k).wait_send()
        for t in range(SITES - 1):
            for j in range(REACH - t):
                @pl.when(swaps(t, j))
                def _():
                    swap(t, j).wait_send()
        for pair in range(channels // 2):
            last_copy(parity, pair).wait_send()
        for kind in range(4):
            @pl.loop(0, places)
            def _(step):
                @pl.when(jnp.logical_not(sum_self(kind, step)))
                def _():
                    sum_copy(kind, step).wait_send()

    @pl.when(role == 2)
    def _():
        for k in range(REACH):
            for i in range(held):
                if k < REACH - 1:
                    ring_copy(k, i).wait_send()
                feed(0, k, i, ring.at[k, i], feed_send.at[k, i]).wait_send()

    @pl.when(role == 3)
    def _():
        for i in range(held):
            feed(3, 0, i, ring.at[0, i], feed_send.at[0, i]).wait_send()


def scaled(in_ref, scale_ref, out_ref, final, done_sem):
    channels = final.shape[1]
    factor = scale_ref[0:1, :].reshape(1, 1, final.shape[-1])

    def put(w):
        return pltpu.make_async_copy(final.at[:, w], out_ref.at[:, w], done_sem.at[w])

    for w in range(channels):
        final[:, w] = (in_ref[:, w].astype(F32) * factor).astype(BF16)
        put(w).start()
    for w in range(channels):
        put(w).wait()


def on_device(mps, mpo, mpo_mask, sector_size, pair_live):
    places = lax.axis_size("tensor")
    held, width = mps.shape[1], mps.shape[-1]
    channels = mpo.shape[1]
    vmem, dma = pltpu.VMEM, pltpu.SemaphoreType.DMA
    in_vmem, in_smem = pl.BlockSpec(memory_space=pltpu.VMEM), pl.BlockSpec(memory_space=pltpu.SMEM)
    result = (held, channels, width, width)
    environment, scale = pl.pallas_call(
        kernel,
        out_shape=(
            jax.ShapeDtypeStruct(result, BF16),
            jax.ShapeDtypeStruct((8, width), F32),
        ),
        in_specs=[pl.BlockSpec(memory_space=pl.ANY), in_vmem, in_vmem, in_smem, in_smem],
        out_specs=(in_vmem, in_vmem),
        scratch_shapes=[
            vmem((held, PHYS, width, width), BF16),
            vmem((REACH, held, PHYS, width, width), BF16),
            vmem((SITES, REACH, PHYS, width, width), BF16),
            vmem((SITES, 2, REACH, channels, width, width), BF16),
            vmem((SITES - 1, channels * 8, channels * 8), BF16),
            vmem((SITES - 1, channels * 16, channels * 16), BF16),
            vmem((SITES - 1, channels * 8, channels * 8), BF16),
            vmem((len(PAIRS), channels, 8, width), F32),
            vmem((channels * PHYS * PHYS, width), F32),
            vmem((channels // 2, PHYS * width, 2 * width), BF16),
            vmem((2, SITES, 8, width), F32),
            vmem((1, width), F32),
            vmem((2 * places, 1, width), F32),
            dma,
            dma((REACH, held)),
            dma((REACH, held)),
            dma((REACH, held)),
            dma((SITES, REACH)),
            dma((SITES, REACH)),
            dma((SITES, REACH)),
            dma((SITES, REACH)),
            dma((channels // 2,)),
            dma((held, channels // 2)),
            dma((SITES, places)),
            dma,
            pltpu.SemaphoreType.REGULAR((len(ROUNDS),)),
        ],
        compiler_params=pltpu.CompilerParams(
            collective_id=0, has_side_effects=True, vmem_limit_bytes=48 * 1024 * 1024
        ),
    )(
        mps[0],
        jnp.transpose(mpo, (0, 1, 3, 4, 2)),
        jnp.transpose(mpo_mask, (1, 0, 2)),
        sector_size,
        pair_live,
    )
    return pl.pallas_call(
        scaled,
        out_shape=jax.ShapeDtypeStruct(result, BF16),
        in_specs=[in_vmem, in_vmem],
        out_specs=pl.BlockSpec(memory_space=pl.ANY),
        scratch_shapes=[vmem(result, BF16), dma((channels,))],
    )(environment, scale)[None]


def solution(mesh):
    in_specs = (
        P("site", "tensor", None, None, None),
        P(),
        P(),
        P("site", "tensor"),
        P("site", "tensor", None),
    )
    out_specs = P("site", "tensor", None, None, None)
    return jax.shard_map(
        on_device, mesh=mesh, in_specs=in_specs, out_specs=out_specs, check_vma=False
    )
```

```python
import jax
import jax.numpy as jnp
from jax import lax
from jax.experimental import pallas as pl
from jax.experimental.pallas import tpu as pltpu
from jax.sharding import PartitionSpec as P

SITES = 4
PHYS = 4
CHARGE = (0, 1, 1, 2)
PAIRS = (0, 5, 6, 9, 10, 15)
ROUNDS = (1, 2, 4, 1)
MESH = pl.DeviceIdType.MESH
EPSILON = 1e-06
SMALL = 2.0**-12
F32 = jnp.float32
BF16 = jnp.bfloat16
REACH = 4


def nt(a, b):
    return lax.dot_general(a, b, (((1,), (1,)), ((), ())), preferred_element_type=F32)


def nn(a, b):
    return lax.dot_general(a, b, (((1,), (0,)), ((), ())), preferred_element_type=F32)


def ids(rows, columns, axis):
    return lax.broadcasted_iota(jnp.int32, (rows, columns), axis)


def table_of(p, mpo_ref, mask_ref, table):
    channels = mask_ref.shape[0]
    table[...] = jnp.zeros_like(table)
    for w in range(channels):
        keep = mask_ref[w, p : p + 1, :] > 0
        for s in range(PHYS):
            tile = jnp.where(keep, mpo_ref[p, w, s].astype(F32), 0.0)
            at = (w * PHYS + s) * PHYS
            table[at : at + PHYS, :channels] = tile
    return table[...].astype(BF16)


def one_hot(condition):
    return jnp.where(condition, 1.0, 0.0).astype(BF16)


def spread(table, channels, first, count):
    one = channels * 8
    size, depth = count * one, table.shape[0]

    def split(x):
        state = jnp.where(x >= one, 1, 0)
        return state + first, (x - state * one) // 8

    _, channel_of_column = split(ids(table.shape[1], size, 1))
    wide = nn(table, one_hot(ids(table.shape[1], size, 0) == channel_of_column))
    state_of_column, _ = split(ids(depth, size, 1))
    wide = jnp.where(ids(depth, size, 0) % PHYS == state_of_column, wide, 0.0).astype(BF16)
    state_of_row, channel_of_row = split(ids(size, depth, 0))
    entry = ids(size, depth, 1)
    pick = one_hot(entry // PHYS == channel_of_row * PHYS + state_of_row)
    full = nn(pick, wide)
    return jnp.where(ids(size, size, 0) % 8 == ids(size, size, 1) % 8, full, 0.0).astype(BF16)


def edge_of(table, channels, coef):
    depth, lanes = table.shape
    last = nn(table, one_hot(ids(lanes, lanes, 0) == channels - 1)).astype(BF16)
    rows = channels * 8
    for i, code in enumerate(PAIRS):
        pick = one_hot(ids(rows, depth, 1) == ids(rows, depth, 0) // 8 * PHYS * PHYS + code)
        coef[i] = nn(pick, last).reshape(channels, 8, lanes)


def kernel(
    m_ref, mpo_in, mask_in, size_in, live_in, out_ref, scale_ref,
    mpo_ref, mask_ref, size_ref, live_ref, raw, ring, m_all, r_all, mix_low, mix_mid, mix_top, coef, table, mixed, squares, mine, heard,
    load_sem, ring_send, ring_recv, feed_send, feed_recv, pass_send, swap_send, swap_recv,
    sum_send, sum_recv, round_sem,
):
    site, place = lax.axis_index("site"), lax.axis_index("tensor")
    sites, places = lax.axis_size("site"), lax.axis_size("tensor")
    role = site % SITES
    hub = jnp.where(role == 3, (site + 1) % sites, site - role)
    channels, width = r_all.shape[3], r_all.shape[4]
    held = m_ref.shape[0]
    far = hub + 2
    end = (hub + sites - 1) % sites
    parity = jnp.where(role == 1, 1, 0)
    partner = hub + 1 - parity
    works = role < 2

    def at(step):
        return lax.rem(place + step + places, places)

    loads = [
        pltpu.make_async_copy(src, dst, load_sem.at[i])
        for i, (src, dst) in enumerate((
            (m_ref, raw), (size_in, size_ref), (live_in, live_ref),
            (mpo_in, mpo_ref), (mask_in, mask_ref),
        ))
    ]
    for load in loads:
        load.start()
    barrier = pltpu.get_barrier_semaphore()

    def greet(*targets):
        for site_to, place_to in targets:
            pl.semaphore_signal(barrier, inc=1, device_id=(site_to, place_to), device_id_type=MESH)

    @pl.when(works)
    def _():
        greet((far, place), (end, place), (partner, place), (site, at(1)), (site, at(-1)))

    @pl.when(role == 2)
    def _():
        greet((hub, place), (hub + 1, place), (site, at(1)), (site, at(-1)))

    @pl.when(role == 3)
    def _():
        greet((hub, place), (hub + 1, place))

    for load in loads:
        load.wait()
    for i in range(held):
        sector = place * held + i
        for s in range(PHYS):
            charge = CHARGE[s]
            live = (live_ref[0, i, charge] > 0) & (sector + charge < places * held)
            bound = jnp.where(live, size_ref[0, i], 0)
            block = jnp.where(ids(width, width, 0) < bound, raw[i, s].astype(F32), 0.0)
            ring[0, i, s] = block.astype(BF16)

    def remote(src, dst, send, recv, site_to, place_to):
        return pltpu.make_async_remote_copy(
            src_ref=src, dst_ref=dst, send_sem=send, recv_sem=recv,
            device_id=(site_to, place_to), device_id_type=MESH,
        )

    def half(k, i, h):
        return ring.at[k, i, pl.ds(2 * h, 2)]

    def ring_copy(k, i, h):
        return remote(
            half(k, i, h), half(k + 1, i, h), ring_send.at[k, i, h], ring_recv.at[k + 1, i, h],
            site, at(-1),
        )

    def ring_wait(k, i, h):
        remote(
            half(k, i, h), half(k, i, h), ring_send.at[0, 0, 0], ring_recv.at[k, i, h],
            site, at(-1),
        ).wait_recv()

    def feed_half(k, i, h):
        return remote(
            half(k, i, h), m_all.at[0, k, pl.ds(2 * h, 2)], feed_send.at[k, i],
            feed_recv.at[0, k], hub + i, place,
        )

    def feed(turn, k, i, source, send):
        return remote(
            source, m_all.at[turn, k], send, feed_recv.at[turn, k], hub + i, place
        )

    def feed_wait(turn, k):
        part = m_all.at[turn, k]
        remote(
            part, part, pass_send.at[0, 0], feed_recv.at[turn, k], partner, place
        ).wait_recv()

    def pass_on(turn, k):
        return remote(
            m_all.at[turn, k], m_all.at[turn, k + 1], pass_send.at[turn, k],
            feed_recv.at[turn, k + 1], site, at(-1),
        )

    def pass_first(turn):
        return remote(
            ring.at[0, parity], m_all.at[turn, 1], pass_send.at[turn, 0],
            feed_recv.at[turn, 1], site, at(-1),
        )

    def start(blocks, target, slot):
        low = blocks[0]
        mid = blocks[1:3].reshape(2 * width, width)
        top = blocks[3]
        step = 32
        total = jnp.zeros((8, width), F32)
        for row in range(0, width, step):
            g0 = nt(low[row : row + step], low)
            g1 = nt(mid[row : row + step], mid)
            g2 = nt(mid[width + row : width + row + step], mid)
            g3 = nt(top[row : row + step], top)
            parts = (g0, g1[:, :width], g1[:, width:], g2[:, :width], g2[:, width:], g3)
            parts = [x.reshape(step // 8, 8, width) for x in parts]
            for w in range(channels):
                block = parts[0] * coef[0, w][None]
                for i in range(1, len(PAIRS)):
                    block = block + parts[i] * coef[i, w][None]
                target[w, row : row + step, :] = block.reshape(step, width).astype(BF16)
                small = block * SMALL
                total = total + jnp.sum(small * small, axis=0)
        squares[slot, 0] += total

    def swap_part(turn, j, part):
        last = turn == SITES - 1
        arrival = jnp.where(last, parity, j)
        return remote(
            part, part, swap_send.at[turn, j], swap_recv.at[turn, arrival],
            jnp.where(last, end, partner), place,
        )

    def swap(turn, j):
        return swap_part(turn, j, r_all.at[turn, parity, j])

    def swap_pair(turn, j, pair):
        @pl.when(swaps(turn, j))
        def _():
            swap_part(turn, j, r_all.at[turn, parity, j, pl.ds(2 * pair, 2)]).start()

    def advance(turn, j):
        prev = turn - 1
        low = m_all[turn, j, 0]
        mid = m_all[turn, j, 1:3].reshape(2 * width, width)
        top = m_all[turn, j, 3]
        step = 32

        def pairs(x):
            y = x.reshape(channels, step // 8, 8, width)
            cut = lambda i: y[:, i].reshape(channels * 8, width)
            return [
                jnp.concatenate([cut(2 * j), cut(2 * j + 1)], axis=1).astype(BF16)
                for j in range(step // 16)
            ]

        k_low, k_mid, k_top = mix_low[prev], mix_mid[prev], mix_top[prev]
        for row in range(0, width, step):
            def rows_of(which, slot):
                rows = r_all[prev, which, slot, :, row : row + step, :]
                return rows.reshape(channels * step, width)

            x0 = pairs(nt(rows_of(parity, j), low))
            x12 = nt(rows_of(1 - parity, j + parity), mid)
            x1, x2 = pairs(x12[:, :width]), pairs(x12[:, width:])
            x3 = pairs(nt(rows_of(parity, j + 1), top))
            for i in range(step // 16):
                y0 = nn(k_low, x0[i])
                y12 = nn(k_mid, jnp.concatenate([x1[i], x2[i]], axis=0))
                y3 = nn(k_top, x3[i])
                for s, y in ((0, y0), (1, y12[: channels * 8]), (2, y12[channels * 8 :]), (3, y3)):
                    z = y.reshape(channels, 8, 2 * width)
                    at_row = s * width + row + 16 * i
                    for w in range(channels):
                        both = jnp.concatenate([z[w, :, :width], z[w, :, width:]], axis=0)
                        lane = (w % 2) * width
                        mixed[w // 2, at_row : at_row + 16, lane : lane + width] = both.astype(BF16)
        wide = jnp.concatenate([low, mid[:width], mid[width:], top], axis=1)
        total = jnp.zeros((8, 2 * width), F32)
        for pair in range(channels // 2):
            block = nn(wide, mixed[pair])
            r_all[turn, parity, j, 2 * pair] = block[:, :width].astype(BF16)
            r_all[turn, parity, j, 2 * pair + 1] = block[:, width:].astype(BF16)
            small = block * SMALL
            total = total + jnp.sum((small * small).reshape(width // 8, 8, 2 * width), axis=0)
            if pair > 0:
                swap_pair(turn, j, pair - 1)
        slot = (j >= 1).astype(jnp.int32)
        squares[slot, turn] += total[:, :width] + total[:, width:]
        swap_pair(turn, j, channels // 2 - 1)

    def swap_wait(turn, j):
        part = r_all.at[turn, 1 - parity, j]
        remote(
            part, part, swap_send.at[turn, j], swap_recv.at[turn, j], partner, place
        ).wait_recv()

    def swaps(turn, j):
        even = (parity == 0) & ((j >= 1) | (turn == 1))
        odd = (parity == 1) & (j <= 2 - turn)
        return (turn == 3) | even | odd

    def tell(i):
        for step in (ROUNDS[i], -ROUNDS[i]):
            pl.semaphore_signal(
                round_sem.at[i], inc=1, device_id=(site, at(step)), device_id_type=MESH
            )

    def told(i):
        pl.semaphore_wait(round_sem.at[i], 2)

    targets = (end, hub, hub + 1, far)

    def sum_copy(kind, step):
        return remote(
            mine, heard.at[parity * places + place], sum_send.at[kind, step], sum_recv,
            targets[kind], at(step),
        )

    def sum_self(kind, step):
        return (step == 0) & (kind == parity + 1)

    @pl.when(role == 2)
    def _():
        pl.semaphore_wait(barrier, 4)

        @pl.loop(0, REACH)
        def _(k):
            for i in range(held):
                for h in range(2):
                    @pl.when(k > 0)
                    def _():
                        ring_wait(k, i, h)

                    @pl.when(k < REACH - 1)
                    def _():
                        ring_copy(k, i, h).start()

                    feed_half(k, i, h).start()

        edge_of(table_of(SITES - 1, mpo_ref, mask_ref, table), channels, coef)
        squares[...] = jnp.zeros_like(squares)

        @pl.loop(0, held)
        def _(i):
            start(ring.at[0, i], r_all.at[0, i, 0], 1)

    @pl.when(role == 3)
    def _():
        pl.semaphore_wait(barrier, 2)
        for i in range(held):
            feed(3, 0, i, ring.at[0, i], feed_send.at[0, i]).start()

    @pl.when(works)
    def _():
        home = 2 - parity
        pl.semaphore_wait(barrier, 5)
        tell(0)
        feed(home, 0, 1 - parity, ring.at[0, 1 - parity], feed_send.at[0, 0]).start()
        pass_first(home).start()
        m_all[home, 0] = ring[0, parity]
        edge_of(table_of(SITES - 1, mpo_ref, mask_ref, table), channels, coef)
        squares[...] = jnp.zeros_like(squares)
        feed_wait(1 + parity, 0)
        pass_on(1 + parity, 0).start()
        told(0)
        tell(1)
        for turn in range(1, SITES):
            found = table_of(SITES - 1 - turn, mpo_ref, mask_ref, table)
            mix_low[turn - 1] = spread(found, channels, 0, 1)
            mix_mid[turn - 1] = spread(found, channels, 1, 2)
            mix_top[turn - 1] = spread(found, channels, 3, 1)
        feed_wait(1, 1)
        pass_on(1, 1).start()
        told(1)
        tell(2)

        @pl.loop(0, REACH)
        def _(k):
            feed_wait(0, k)
            start(m_all.at[0, k], r_all.at[0, parity, k], (k >= 1).astype(jnp.int32))

            @pl.when(swaps(0, k))
            def _():
                swap(0, k).start()

            @pl.loop(1, k + 1)
            def _(t):
                @pl.when(k == REACH - 1)
                def _():
                    feed_wait(t, k - t)

                swap_wait(t - 1, k - t + parity)
                advance(t, k - t)

            @pl.when(k == 1)
            def _():
                told(2)
                tell(3)

        lane = ids(1, width, 1)
        row = jnp.zeros((1, width), F32)
        for t in range(SITES):
            row = row + jnp.where(lane == t, jnp.sum(squares[0, t]), 0.0)
        mine[...] = row
        heard[parity * places + place] = row
        told(3)

        for kind in range(4):
            @pl.loop(0, places)
            def _(step):
                @pl.when(jnp.logical_not(sum_self(kind, step)))
                def _():
                    sum_copy(kind, step).start()

    def heard_all(count):
        part = heard.at[pl.ds(0, count)]
        remote(part, part, sum_send.at[0, 0], sum_recv, site, at(1)).wait_recv()

    @pl.when(role == 3)
    def _():
        for i in range(held):
            part = r_all.at[3, i, 0]
            remote(
                part, part, swap_send.at[3, 0], swap_recv.at[3, i], hub + i, place
            ).wait_recv()

    @pl.when(role == 1)
    def _():
        swap_wait(1, 0)

    @pl.when(works)
    def _():
        heard_all(2 * places - 1)

    @pl.when(role >= 2)
    def _():
        heard_all(2 * places)

    turn = jnp.where(role == 3, 3, 2 - role)
    sums = jnp.sum(heard[...].reshape(2 * places, width), axis=0, keepdims=True)
    entries = float(places * held * channels * width * width)
    unit = jnp.ones((1, 1), F32)
    chosen = unit
    for t in range(SITES):
        square = sums[:, t : t + 1] * (1.0 / (SMALL * SMALL * entries)) * unit * unit
        unit = unit * lax.rsqrt(square + EPSILON)
        chosen = jnp.where(turn == t, unit, chosen)
    scale_ref[...] = jnp.broadcast_to(chosen, scale_ref.shape)
    for i in range(held):
        out_ref[i] = r_all[turn, i, 0]

    @pl.when(works)
    def _():
        home = 2 - parity
        feed(home, 0, 1 - parity, ring.at[0, 1 - parity], feed_send.at[0, 0]).wait_send()
        for t, k in ((1, 0), (1, 1), (2, 0)):
            pass_on(t, k).wait_send()
        for t in range(SITES):
            for j in range(REACH - t):
                @pl.when(swaps(t, j))
                def _():
                    swap(t, j).wait_send()
        for kind in range(4):
            @pl.loop(0, places)
            def _(step):
                @pl.when(jnp.logical_not(sum_self(kind, step)))
                def _():
                    sum_copy(kind, step).wait_send()

    @pl.when(role == 2)
    def _():
        for k in range(REACH):
            for i in range(held):
                for h in range(2):
                    if k < REACH - 1:
                        ring_copy(k, i, h).wait_send()
                feed(0, k, i, ring.at[k, i], feed_send.at[k, i]).wait_send()

    @pl.when(role == 3)
    def _():
        for i in range(held):
            feed(3, 0, i, ring.at[0, i], feed_send.at[0, i]).wait_send()


def scaled(in_ref, scale_ref, out_ref, final, done_sem):
    channels = final.shape[1]
    factor = scale_ref[0:1, :].reshape(1, 1, final.shape[-1])

    def put(w):
        return pltpu.make_async_copy(final.at[:, w], out_ref.at[:, w], done_sem.at[w])

    for w in range(channels):
        final[:, w] = (in_ref[:, w].astype(F32) * factor).astype(BF16)
        put(w).start()
    for w in range(channels):
        put(w).wait()


def on_device(mps, mpo, mpo_mask, sector_size, pair_live):
    places = lax.axis_size("tensor")
    held, width = mps.shape[1], mps.shape[-1]
    channels = mpo.shape[1]
    vmem, dma = pltpu.VMEM, pltpu.SemaphoreType.DMA
    in_vmem, in_hbm = pl.BlockSpec(memory_space=pltpu.VMEM), pl.BlockSpec(memory_space=pltpu.HBM)
    result = (held, channels, width, width)
    environment, scale = pl.pallas_call(
        kernel,
        out_shape=(
            jax.ShapeDtypeStruct(result, BF16),
            jax.ShapeDtypeStruct((8, width), F32),
        ),
        in_specs=[in_hbm] * 5,
        out_specs=(in_vmem, in_vmem),
        scratch_shapes=[
            vmem((SITES, channels, PHYS, PHYS, channels), BF16),
            vmem((channels, SITES, channels), jnp.int32),
            pltpu.SMEM((1, held), jnp.int32),
            pltpu.SMEM((1, held, 3), jnp.int32),
            vmem((held, PHYS, width, width), BF16),
            vmem((REACH, held, PHYS, width, width), BF16),
            vmem((SITES, REACH, PHYS, width, width), BF16),
            vmem((SITES, 2, REACH, channels, width, width), BF16),
            vmem((SITES - 1, channels * 8, channels * 8), BF16),
            vmem((SITES - 1, channels * 16, channels * 16), BF16),
            vmem((SITES - 1, channels * 8, channels * 8), BF16),
            vmem((len(PAIRS), channels, 8, width), F32),
            vmem((channels * PHYS * PHYS, width), F32),
            vmem((channels // 2, PHYS * width, 2 * width), BF16),
            vmem((2, SITES, 8, width), F32),
            vmem((1, width), F32),
            vmem((2 * places, 1, width), F32),
            dma((5,)),
            dma((REACH, held, 2)),
            dma((REACH, held, 2)),
            dma((REACH, held)),
            dma((SITES, REACH)),
            dma((SITES, REACH)),
            dma((SITES, REACH)),
            dma((SITES, REACH)),
            dma((SITES, places)),
            dma,
            pltpu.SemaphoreType.REGULAR((len(ROUNDS),)),
        ],
        compiler_params=pltpu.CompilerParams(
            collective_id=0, has_side_effects=True, vmem_limit_bytes=48 * 1024 * 1024
        ),
    )(
        *[
            pltpu.with_memory_space_constraint(x, pltpu.HBM)
            for x in (
                mps[0],
                jnp.transpose(mpo, (0, 1, 3, 4, 2)),
                jnp.transpose(mpo_mask, (1, 0, 2)),
                sector_size,
                pair_live,
            )
        ]
    )
    return pl.pallas_call(
        scaled,
        out_shape=jax.ShapeDtypeStruct(result, BF16),
        in_specs=[in_vmem, in_vmem],
        out_specs=pl.BlockSpec(memory_space=pl.ANY),
        scratch_shapes=[vmem(result, BF16), dma((channels,))],
        compiler_params=pltpu.CompilerParams(vmem_limit_bytes=4 * 1024 * 1024),
    )(environment, scale)[None]


def solution(mesh):
    in_specs = (
        P("site", "tensor", None, None, None),
        P(),
        P(),
        P("site", "tensor"),
        P("site", "tensor", None),
    )
    out_specs = P("site", "tensor", None, None, None)
    return jax.shard_map(
        on_device, mesh=mesh, in_specs=in_specs, out_specs=out_specs, check_vma=False
    )
```

```python
import jax
import jax.numpy as jnp
from jax import lax
from jax.experimental import pallas as pl
from jax.experimental.pallas import tpu as pltpu
from jax.sharding import PartitionSpec as P

SITES = 4
PHYS = 4
CHARGE = (0, 1, 1, 2)
PAIRS = (0, 5, 6, 9, 10, 15)
ROUNDS = (1, 2, 4, 1)
MESH = pl.DeviceIdType.MESH
EPSILON = 1e-06
SMALL = 2.0**-12
F32 = jnp.float32
BF16 = jnp.bfloat16
REACH = 4


def nt(a, b):
    return lax.dot_general(a, b, (((1,), (1,)), ((), ())), preferred_element_type=F32)


def nn(a, b):
    return lax.dot_general(a, b, (((1,), (0,)), ((), ())), preferred_element_type=F32)


def ids(rows, columns, axis):
    return lax.broadcasted_iota(jnp.int32, (rows, columns), axis)


def table_of(p, mpo_ref, mask_ref, table):
    channels = mask_ref.shape[0]
    table[...] = jnp.zeros_like(table)
    for w in range(channels):
        keep = mask_ref[w, p : p + 1, :] > 0
        for s in range(PHYS):
            tile = jnp.where(keep, mpo_ref[p, w, s].astype(F32), 0.0)
            at = (w * PHYS + s) * PHYS
            table[at : at + PHYS, :channels] = tile
    return table[...].astype(BF16)


def one_hot(condition):
    return jnp.where(condition, 1.0, 0.0).astype(BF16)


def spread(table, channels, first, count):
    one = channels * 8
    size, depth = count * one, table.shape[0]

    def split(x):
        state = jnp.where(x >= one, 1, 0)
        return state + first, (x - state * one) // 8

    _, channel_of_column = split(ids(table.shape[1], size, 1))
    wide = nn(table, one_hot(ids(table.shape[1], size, 0) == channel_of_column))
    state_of_column, _ = split(ids(depth, size, 1))
    wide = jnp.where(ids(depth, size, 0) % PHYS == state_of_column, wide, 0.0).astype(BF16)
    state_of_row, channel_of_row = split(ids(size, depth, 0))
    entry = ids(size, depth, 1)
    pick = one_hot(entry // PHYS == channel_of_row * PHYS + state_of_row)
    full = nn(pick, wide)
    return jnp.where(ids(size, size, 0) % 8 == ids(size, size, 1) % 8, full, 0.0).astype(BF16)


def edge_of(table, channels, coef):
    depth, lanes = table.shape
    last = nn(table, one_hot(ids(lanes, lanes, 0) == channels - 1)).astype(BF16)
    rows = channels * 8
    for i, code in enumerate(PAIRS):
        pick = one_hot(ids(rows, depth, 1) == ids(rows, depth, 0) // 8 * PHYS * PHYS + code)
        coef[i] = nn(pick, last).reshape(channels, 8, lanes)


def kernel(
    m_ref, mpo_in, mask_in, size_in, live_in, out_ref, scale_ref,
    mpo_ref, mask_ref, size_ref, live_ref, raw, ring, m_all, r_all, mix_low, mix_mid, mix_top, coef, table, mixed, partial, squares, mine, heard,
    load_sem, ring_send, ring_recv, feed_send, feed_recv, pass_send, swap_send, swap_recv,
    sum_send, sum_recv, round_sem,
):
    site, place = lax.axis_index("site"), lax.axis_index("tensor")
    sites, places = lax.axis_size("site"), lax.axis_size("tensor")
    role = site % SITES
    hub = jnp.where(role == 3, (site + 1) % sites, site - role)
    channels, width = r_all.shape[3], r_all.shape[4]
    held = m_ref.shape[0]
    far = hub + 2
    end = (hub + sites - 1) % sites
    parity = jnp.where(role == 1, 1, 0)
    partner = hub + 1 - parity
    works = role < 2

    def at(step):
        return lax.rem(place + step + places, places)

    loads = [
        pltpu.make_async_copy(src, dst, load_sem.at[i])
        for i, (src, dst) in enumerate((
            (m_ref, raw), (size_in, size_ref), (live_in, live_ref),
            (mpo_in, mpo_ref), (mask_in, mask_ref),
        ))
    ]
    for load in loads:
        load.start()
    barrier = pltpu.get_barrier_semaphore()

    def greet(*targets):
        for site_to, place_to in targets:
            pl.semaphore_signal(barrier, inc=1, device_id=(site_to, place_to), device_id_type=MESH)

    @pl.when(works)
    def _():
        greet((far, place), (far, at(1)), (end, place), (partner, place))
        greet((site, at(1)), (site, at(-1)))

    @pl.when(role == 2)
    def _():
        greet((hub, place), (hub + 1, place), (hub, at(-1)), (hub + 1, at(-1)))
        greet((site, at(1)), (site, at(-1)))

    @pl.when(role == 3)
    def _():
        greet((hub, place), (hub + 1, place))

    for load in loads[:3]:
        load.wait()
    for i in range(held):
        sector = place * held + i
        for s in range(PHYS):
            charge = CHARGE[s]
            live = (live_ref[0, i, charge] > 0) & (sector + charge < places * held)
            bound = jnp.where(live, size_ref[0, i], 0)
            block = jnp.where(ids(width, width, 0) < bound, raw[i, s].astype(F32), 0.0)
            ring[0, i, s] = block.astype(BF16)

    def load_weights():
        for load in loads[3:]:
            load.wait()

    def remote(src, dst, send, recv, site_to, place_to):
        return pltpu.make_async_remote_copy(
            src_ref=src, dst_ref=dst, send_sem=send, recv_sem=recv,
            device_id=(site_to, place_to), device_id_type=MESH,
        )

    def half(k, i, h):
        return ring.at[k, i, pl.ds(2 * h, 2)]

    def ring_copy(k, i, h):
        return remote(
            half(k, i, h), half(k + 1, i, h), ring_send.at[k, i, h], ring_recv.at[k + 1, i, h],
            site, at(-1),
        )

    def ring_wait(k, i, h):
        remote(
            half(k, i, h), half(k, i, h), ring_send.at[0, 0, 0], ring_recv.at[k, i, h],
            site, at(-1),
        ).wait_recv()

    def feed_far(i, h):
        return remote(
            half(2, i, h), m_all.at[0, REACH - 1, pl.ds(2 * h, 2)], feed_send.at[REACH - 1, i],
            feed_recv.at[0, REACH - 1], hub + i, at(-1),
        )

    def feed_half(k, i, h):
        return remote(
            half(k, i, h), m_all.at[0, k, pl.ds(2 * h, 2)], feed_send.at[k, i],
            feed_recv.at[0, k], hub + i, place,
        )

    def feed(turn, k, i, source, send):
        return remote(
            source, m_all.at[turn, k], send, feed_recv.at[turn, k], hub + i, place
        )

    def feed_wait(turn, k):
        part = m_all.at[turn, k]
        remote(
            part, part, pass_send.at[0, 0], feed_recv.at[turn, k], partner, place
        ).wait_recv()

    def pass_on(turn, k):
        return remote(
            m_all.at[turn, k], m_all.at[turn, k + 1], pass_send.at[turn, k],
            feed_recv.at[turn, k + 1], site, at(-1),
        )

    def pass_first(turn):
        return remote(
            ring.at[0, parity], m_all.at[turn, 1], pass_send.at[turn, 0],
            feed_recv.at[turn, 1], site, at(-1),
        )

    def start(blocks, target, slot):
        low = blocks[0]
        mid = blocks[1:3].reshape(2 * width, width)
        top = blocks[3]
        step = 32
        total = jnp.zeros((8, width), F32)
        for row in range(0, width, step):
            g0 = nt(low[row : row + step], low)
            g1 = nt(mid[row : row + step], mid)
            g2 = nt(mid[width + row : width + row + step], mid)
            g3 = nt(top[row : row + step], top)
            parts = (g0, g1[:, :width], g1[:, width:], g2[:, :width], g2[:, width:], g3)
            parts = [x.reshape(step // 8, 8, width) for x in parts]
            for w in range(channels):
                block = parts[0] * coef[0, w][None]
                for i in range(1, len(PAIRS)):
                    block = block + parts[i] * coef[i, w][None]
                target[w, row : row + step, :] = block.reshape(step, width).astype(BF16)
                small = block * SMALL
                total = total + jnp.sum(small * small, axis=0)
        squares[slot, 0] += total

    def swap_part(turn, j, part):
        last = turn == SITES - 1
        arrival = jnp.where(last, parity, j)
        return remote(
            part, part, swap_send.at[turn, j], swap_recv.at[turn, arrival],
            jnp.where(last, end, partner), place,
        )

    def swap(turn, j):
        return swap_part(turn, j, r_all.at[turn, parity, j])

    def swap_pair(turn, j, pair):
        @pl.when(swaps(turn, j) & (turn < SITES - 1))
        def _():
            swap_part(turn, j, r_all.at[turn, parity, j, pl.ds(2 * pair, 2)]).start()

    def advance(turn, j, parts=(0, 1, 2), first=True, last=True):
        prev = turn - 1
        low = m_all[turn, j, 0]
        mid = m_all[turn, j, 1:3].reshape(2 * width, width)
        top = m_all[turn, j, 3]
        step = 32

        def pairs(x):
            y = x.reshape(channels, step // 8, 8, width)
            cut = lambda i: y[:, i].reshape(channels * 8, width)
            return [
                jnp.concatenate([cut(2 * j), cut(2 * j + 1)], axis=1).astype(BF16)
                for j in range(step // 16)
            ]

        for row in range(0, width, step):
            def rows_of(which, slot):
                rows = r_all[prev, which, slot, :, row : row + step, :]
                return rows.reshape(channels * step, width)

            def put(s, i, y):
                z = y.reshape(channels, 8, 2 * width)
                at_row = s * width + row + 16 * i
                for w in range(channels):
                    both = jnp.concatenate([z[w, :, :width], z[w, :, width:]], axis=0)
                    lane = (w % 2) * width
                    mixed[w // 2, at_row : at_row + 16, lane : lane + width] = both.astype(BF16)

            if 0 in parts:
                x0 = pairs(nt(rows_of(parity, j), low))
            if 1 in parts:
                x12 = nt(rows_of(1 - parity, j + parity), mid)
                x1, x2 = pairs(x12[:, :width]), pairs(x12[:, width:])
            if 2 in parts:
                x3 = pairs(nt(rows_of(parity, j + 1), top))
            for i in range(step // 16):
                if 0 in parts:
                    put(0, i, nn(mix_low[prev], x0[i]))
                if 1 in parts:
                    y12 = nn(mix_mid[prev], jnp.concatenate([x1[i], x2[i]], axis=0))
                    put(1, i, y12[: channels * 8])
                    put(2, i, y12[channels * 8 :])
                if 2 in parts:
                    put(3, i, nn(mix_top[prev], x3[i]))
        wide = {0: [low], 1: [mid[:width], mid[width:]], 2: [top]}
        wide = jnp.concatenate([m for part in parts for m in wide[part]], axis=1)
        start_row = {0: 0, 1: width, 2: 3 * width}[parts[0]]
        total = jnp.zeros((8, 2 * width), F32)
        for pair in range(channels // 2):
            block = nn(wide, mixed[pair, start_row : start_row + wide.shape[1]])
            if not first:
                block = block + partial[prev, pair]
            if not last:
                partial[prev, pair] = block
                continue
            r_all[turn, parity, j, 2 * pair] = block[:, :width].astype(BF16)
            r_all[turn, parity, j, 2 * pair + 1] = block[:, width:].astype(BF16)
            small = block * SMALL
            total = total + jnp.sum((small * small).reshape(width // 8, 8, 2 * width), axis=0)
            if pair > 0:
                swap_pair(turn, j, pair - 1)
        if last:
            slot = (j >= 1).astype(jnp.int32)
            squares[slot, turn] += total[:, :width] + total[:, width:]
            swap_pair(turn, j, channels // 2 - 1)

    def swap_wait(turn, j):
        part = r_all.at[turn, 1 - parity, j]
        remote(
            part, part, swap_send.at[turn, j], swap_recv.at[turn, j], partner, place
        ).wait_recv()

    def swaps(turn, j):
        even = (parity == 0) & ((j >= 1) | (turn == 1))
        odd = (parity == 1) & (j <= 2 - turn)
        return (turn == 3) | even | odd

    def tell(i):
        for step in (ROUNDS[i], -ROUNDS[i]):
            pl.semaphore_signal(
                round_sem.at[i], inc=1, device_id=(site, at(step)), device_id_type=MESH
            )

    def told(i):
        pl.semaphore_wait(round_sem.at[i], 2)

    targets = (end, hub, hub + 1, far)

    def sum_copy(kind, step):
        return remote(
            mine, heard.at[parity * places + place], sum_send.at[kind, step], sum_recv,
            targets[kind], at(step),
        )

    def sum_self(kind, step):
        return (step == 0) & (kind == parity + 1)

    @pl.when(role == 2)
    def _():
        pl.semaphore_wait(barrier, 6)

        @pl.loop(0, REACH - 1)
        def _(k):
            for i in range(held):
                for h in range(2):
                    @pl.when(k > 0)
                    def _():
                        ring_wait(k, i, h)

                    @pl.when(k < REACH - 2)
                    def _():
                        ring_copy(k, i, h).start()

                    @pl.when(k == REACH - 2)
                    def _():
                        feed_far(i, h).start()

                    feed_half(k, i, h).start()

        load_weights()
        edge_of(table_of(SITES - 1, mpo_ref, mask_ref, table), channels, coef)
        squares[...] = jnp.zeros_like(squares)

        @pl.loop(0, held)
        def _(i):
            start(ring.at[0, i], r_all.at[0, i, 0], 1)

    @pl.when(role == 3)
    def _():
        pl.semaphore_wait(barrier, 2)
        for i in range(held):
            feed(3, 0, i, ring.at[0, i], feed_send.at[0, i]).start()
        load_weights()

    @pl.when(works)
    def _():
        home = 2 - parity
        pl.semaphore_wait(barrier, 6)
        tell(0)
        feed(home, 0, 1 - parity, ring.at[0, 1 - parity], feed_send.at[0, 0]).start()
        pass_first(home).start()
        m_all[home, 0] = ring[0, parity]
        load_weights()
        edge_of(table_of(SITES - 1, mpo_ref, mask_ref, table), channels, coef)
        squares[...] = jnp.zeros_like(squares)
        feed_wait(1 + parity, 0)
        pass_on(1 + parity, 0).start()
        told(0)
        tell(1)
        for turn in range(1, SITES):
            found = table_of(SITES - 1 - turn, mpo_ref, mask_ref, table)
            mix_low[turn - 1] = spread(found, channels, 0, 1)
            mix_mid[turn - 1] = spread(found, channels, 1, 2)
            mix_top[turn - 1] = spread(found, channels, 3, 1)
        feed_wait(1, 1)
        pass_on(1, 1).start()
        told(1)
        tell(2)

        def begin(k):
            feed_wait(0, k)
            start(m_all.at[0, k], r_all.at[0, parity, k], (k >= 1).astype(jnp.int32))

            @pl.when(swaps(0, k))
            def _():
                swap(0, k).start()

        @pl.loop(0, REACH)
        def _(k):
            @pl.when(k == REACH - 1)
            def _():
                @pl.loop(1, SITES)
                def _(t):
                    feed_wait(t, REACH - 1 - t)

                    @pl.when(parity == 0)
                    def _():
                        swap_wait(t - 1, REACH - 1 - t)
                        advance(t, REACH - 1 - t, (0, 1), last=False)

                    @pl.when(parity == 1)
                    def _():
                        advance(t, REACH - 1 - t, (0,), last=False)

            begin(k)

            @pl.when(k < REACH - 1)
            def _():
                @pl.loop(1, k + 1)
                def _(t):
                    swap_wait(t - 1, k - t + parity)
                    advance(t, k - t)

            @pl.when(k == 1)
            def _():
                told(2)
                tell(3)

        @pl.loop(1, SITES)
        def _(t):
            @pl.when(parity == 0)
            def _():
                advance(t, REACH - 1 - t, (2,), first=False)

            @pl.when(parity == 1)
            def _():
                swap_wait(t - 1, REACH - t)
                advance(t, REACH - 1 - t, (1, 2), first=False)

        lane = ids(1, width, 1)
        row = jnp.zeros((1, width), F32)
        for t in range(SITES):
            row = row + jnp.where(lane == t, jnp.sum(squares[0, t]), 0.0)
        mine[...] = row
        heard[parity * places + place] = row
        told(3)

        for kind in range(4):
            @pl.loop(0, places)
            def _(step):
                @pl.when(jnp.logical_not(sum_self(kind, step)))
                def _():
                    sum_copy(kind, step).start()

            if kind == 0:
                swap(SITES - 1, 0).start()

    def heard_all(count):
        part = heard.at[pl.ds(0, count)]
        remote(part, part, sum_send.at[0, 0], sum_recv, site, at(1)).wait_recv()

    @pl.when(role == 3)
    def _():
        for i in range(held):
            part = r_all.at[3, i, 0]
            remote(
                part, part, swap_send.at[3, 0], swap_recv.at[3, i], hub + i, place
            ).wait_recv()

    @pl.when(role == 1)
    def _():
        swap_wait(1, 0)

    @pl.when(works)
    def _():
        heard_all(2 * places - 1)

    @pl.when(role >= 2)
    def _():
        heard_all(2 * places)

    turn = jnp.where(role == 3, 3, 2 - role)
    sums = jnp.sum(heard[...].reshape(2 * places, width), axis=0, keepdims=True)
    entries = float(places * held * channels * width * width)
    unit = jnp.ones((1, 1), F32)
    chosen = unit
    for t in range(SITES):
        square = sums[:, t : t + 1] * (1.0 / (SMALL * SMALL * entries)) * unit * unit
        unit = unit * lax.rsqrt(square + EPSILON)
        chosen = jnp.where(turn == t, unit, chosen)
    scale_ref[...] = jnp.broadcast_to(chosen, scale_ref.shape)
    for i in range(held):
        out_ref[i] = r_all[turn, i, 0]

    @pl.when(works)
    def _():
        home = 2 - parity
        feed(home, 0, 1 - parity, ring.at[0, 1 - parity], feed_send.at[0, 0]).wait_send()
        for t, k in ((1, 0), (1, 1), (2, 0)):
            pass_on(t, k).wait_send()
        for t in range(SITES):
            for j in range(REACH - t):
                @pl.when(swaps(t, j))
                def _():
                    swap(t, j).wait_send()
        for kind in range(4):
            @pl.loop(0, places)
            def _(step):
                @pl.when(jnp.logical_not(sum_self(kind, step)))
                def _():
                    sum_copy(kind, step).wait_send()

    @pl.when(role == 2)
    def _():
        for k in range(REACH):
            for i in range(held):
                for h in range(2):
                    if k < REACH - 2:
                        ring_copy(k, i, h).wait_send()
                feed(0, k, i, ring.at[0, i], feed_send.at[k, i]).wait_send()

    @pl.when(role == 3)
    def _():
        for i in range(held):
            feed(3, 0, i, ring.at[0, i], feed_send.at[0, i]).wait_send()


def scaled(in_ref, scale_ref, out_ref, final, done_sem):
    channels = final.shape[1]
    factor = scale_ref[0:1, :].reshape(1, 1, final.shape[-1])

    def put(w):
        return pltpu.make_async_copy(final.at[:, w], out_ref.at[:, w], done_sem.at[w])

    for w in range(channels):
        final[:, w] = (in_ref[:, w].astype(F32) * factor).astype(BF16)
        put(w).start()
    for w in range(channels):
        put(w).wait()


def on_device(mps, mpo, mpo_mask, sector_size, pair_live):
    places = lax.axis_size("tensor")
    held, width = mps.shape[1], mps.shape[-1]
    channels = mpo.shape[1]
    vmem, dma = pltpu.VMEM, pltpu.SemaphoreType.DMA
    in_vmem, in_hbm = pl.BlockSpec(memory_space=pltpu.VMEM), pl.BlockSpec(memory_space=pltpu.HBM)
    result = (held, channels, width, width)
    environment, scale = pl.pallas_call(
        kernel,
        out_shape=(
            jax.ShapeDtypeStruct(result, BF16),
            jax.ShapeDtypeStruct((8, width), F32),
        ),
        in_specs=[in_hbm] * 5,
        out_specs=(in_vmem, in_vmem),
        scratch_shapes=[
            vmem((SITES, channels, PHYS, PHYS, channels), BF16),
            vmem((channels, SITES, channels), jnp.int32),
            pltpu.SMEM((1, held), jnp.int32),
            pltpu.SMEM((1, held, 3), jnp.int32),
            vmem((held, PHYS, width, width), BF16),
            vmem((REACH - 1, held, PHYS, width, width), BF16),
            vmem((SITES, REACH, PHYS, width, width), BF16),
            vmem((SITES, 2, REACH, channels, width, width), BF16),
            vmem((SITES - 1, channels * 8, channels * 8), BF16),
            vmem((SITES - 1, channels * 16, channels * 16), BF16),
            vmem((SITES - 1, channels * 8, channels * 8), BF16),
            vmem((len(PAIRS), channels, 8, width), F32),
            vmem((channels * PHYS * PHYS, width), F32),
            vmem((channels // 2, PHYS * width, 2 * width), BF16),
            vmem((SITES - 1, channels // 2, width, 2 * width), F32),
            vmem((2, SITES, 8, width), F32),
            vmem((1, width), F32),
            vmem((2 * places, 1, width), F32),
            dma((5,)),
            dma((REACH, held, 2)),
            dma((REACH, held, 2)),
            dma((REACH, held)),
            dma((SITES, REACH)),
            dma((SITES, REACH)),
            dma((SITES, REACH)),
            dma((SITES, REACH)),
            dma((SITES, places)),
            dma,
            pltpu.SemaphoreType.REGULAR((len(ROUNDS),)),
        ],
        compiler_params=pltpu.CompilerParams(
            collective_id=0, has_side_effects=True, vmem_limit_bytes=48 * 1024 * 1024
        ),
    )(
        *[
            pltpu.with_memory_space_constraint(x, pltpu.HBM)
            for x in (
                mps[0],
                jnp.transpose(mpo, (0, 1, 3, 4, 2)),
                jnp.transpose(mpo_mask, (1, 0, 2)),
                sector_size,
                pair_live,
            )
        ]
    )
    return pl.pallas_call(
        scaled,
        out_shape=jax.ShapeDtypeStruct(result, BF16),
        in_specs=[in_vmem, in_vmem],
        out_specs=pl.BlockSpec(memory_space=pl.ANY),
        scratch_shapes=[vmem(result, BF16), dma((channels,))],
        compiler_params=pltpu.CompilerParams(vmem_limit_bytes=4 * 1024 * 1024),
    )(environment, scale)[None]


def solution(mesh):
    in_specs = (
        P("site", "tensor", None, None, None),
        P(),
        P(),
        P("site", "tensor"),
        P("site", "tensor", None),
    )
    out_specs = P("site", "tensor", None, None, None)
    return jax.shard_map(
        on_device, mesh=mesh, in_specs=in_specs, out_specs=out_specs, check_vma=False
    )
```

```python
import jax
import jax.numpy as jnp
from jax import lax
from jax.experimental import pallas as pl
from jax.experimental.pallas import tpu as pltpu
from jax.sharding import PartitionSpec as P

SITES = 4
PHYS = 4
CHARGE = (0, 1, 1, 2)
PAIRS = (0, 5, 6, 9, 10, 15)
ROUNDS = (1, 2, 4, 1)
MESH = pl.DeviceIdType.MESH
EPSILON = 1e-06
SMALL = 2.0**-12
F32 = jnp.float32
BF16 = jnp.bfloat16
REACH = 4


def nt(a, b):
    return lax.dot_general(a, b, (((1,), (1,)), ((), ())), preferred_element_type=F32)


def nn(a, b):
    return lax.dot_general(a, b, (((1,), (0,)), ((), ())), preferred_element_type=F32)


def ids(rows, columns, axis):
    return lax.broadcasted_iota(jnp.int32, (rows, columns), axis)


def table_of(p, mpo_ref, mask_ref, table):
    channels = mask_ref.shape[0]
    table[...] = jnp.zeros_like(table)
    for w in range(channels):
        keep = mask_ref[w, p : p + 1, :] > 0
        for s in range(PHYS):
            tile = jnp.where(keep, mpo_ref[p, w, s].astype(F32), 0.0)
            at = (w * PHYS + s) * PHYS
            table[at : at + PHYS, :channels] = tile
    return table[...].astype(BF16)


def one_hot(condition):
    return jnp.where(condition, 1.0, 0.0).astype(BF16)


def spread(table, channels, first, count):
    one = channels * 8
    size, depth = count * one, table.shape[0]

    def split(x):
        state = jnp.where(x >= one, 1, 0)
        return state + first, (x - state * one) // 8

    _, channel_of_column = split(ids(table.shape[1], size, 1))
    wide = nn(table, one_hot(ids(table.shape[1], size, 0) == channel_of_column))
    state_of_column, _ = split(ids(depth, size, 1))
    wide = jnp.where(ids(depth, size, 0) % PHYS == state_of_column, wide, 0.0).astype(BF16)
    state_of_row, channel_of_row = split(ids(size, depth, 0))
    entry = ids(size, depth, 1)
    pick = one_hot(entry // PHYS == channel_of_row * PHYS + state_of_row)
    full = nn(pick, wide)
    return jnp.where(ids(size, size, 0) % 8 == ids(size, size, 1) % 8, full, 0.0).astype(BF16)


def edge_of(table, channels, coef):
    depth, lanes = table.shape
    last = nn(table, one_hot(ids(lanes, lanes, 0) == channels - 1)).astype(BF16)
    rows = channels * 8
    for i, code in enumerate(PAIRS):
        pick = one_hot(ids(rows, depth, 1) == ids(rows, depth, 0) // 8 * PHYS * PHYS + code)
        coef[i] = nn(pick, last).reshape(channels, 8, lanes)


def kernel(
    m_ref, mpo_in, mask_in, size_in, live_in, out_ref, scale_ref,
    mpo_ref, mask_ref, size_ref, live_ref, raw, ring, m_all, r_all, mix_low, mix_mid, mix_top, coef, table, inner, mixed, squares, mine, heard,
    load_sem, ring_send, ring_recv, feed_send, feed_recv, pass_send, swap_send, swap_recv,
    sum_send, sum_recv, round_sem,
):
    site, place = lax.axis_index("site"), lax.axis_index("tensor")
    sites, places = lax.axis_size("site"), lax.axis_size("tensor")
    role = site % SITES
    hub = jnp.where(role == 3, (site + 1) % sites, site - role)
    channels, width = r_all.shape[3], r_all.shape[4]
    held = m_ref.shape[0]
    far = hub + 2
    end = (hub + sites - 1) % sites
    parity = jnp.where(role == 1, 1, 0)
    partner = hub + 1 - parity
    works = role < 2

    def at(step):
        return lax.rem(place + step + places, places)

    loads = [
        pltpu.make_async_copy(src, dst, load_sem.at[i])
        for i, (src, dst) in enumerate((
            (m_ref, raw), (size_in, size_ref), (live_in, live_ref),
            (mpo_in, mpo_ref), (mask_in, mask_ref),
        ))
    ]
    for load in loads:
        load.start()
    barrier = pltpu.get_barrier_semaphore()

    def greet(*targets):
        for site_to, place_to in targets:
            pl.semaphore_signal(barrier, inc=1, device_id=(site_to, place_to), device_id_type=MESH)

    @pl.when(works)
    def _():
        greet((far, place), (end, place), (partner, place), (site, at(1)), (site, at(-1)))

    @pl.when(role == 2)
    def _():
        greet((hub, place), (hub + 1, place), (site, at(1)), (site, at(-1)))

    @pl.when(role == 3)
    def _():
        greet((hub, place), (hub + 1, place))

    for load in loads[:3]:
        load.wait()
    for i in range(held):
        sector = place * held + i
        for s in range(PHYS):
            charge = CHARGE[s]
            live = (live_ref[0, i, charge] > 0) & (sector + charge < places * held)
            bound = jnp.where(live, size_ref[0, i], 0)
            block = jnp.where(ids(width, width, 0) < bound, raw[i, s].astype(F32), 0.0)
            ring[0, i, s] = block.astype(BF16)

    def load_weights():
        for load in loads[3:]:
            load.wait()

    def remote(src, dst, send, recv, site_to, place_to):
        return pltpu.make_async_remote_copy(
            src_ref=src, dst_ref=dst, send_sem=send, recv_sem=recv,
            device_id=(site_to, place_to), device_id_type=MESH,
        )

    def half(k, i, h):
        return ring.at[k, i, pl.ds(2 * h, 2)]

    def ring_copy(k, i, h):
        return remote(
            half(k, i, h), half(k + 1, i, h), ring_send.at[k, i, h], ring_recv.at[k + 1, i, h],
            site, at(-1),
        )

    def ring_wait(k, i, h):
        remote(
            half(k, i, h), half(k, i, h), ring_send.at[0, 0, 0], ring_recv.at[k, i, h],
            site, at(-1),
        ).wait_recv()

    def feed_half(k, i, h):
        return remote(
            half(k, i, h), m_all.at[0, k, pl.ds(2 * h, 2)], feed_send.at[k, i],
            feed_recv.at[0, k], hub + i, place,
        )

    def feed(turn, k, i, source, send):
        return remote(
            source, m_all.at[turn, k], send, feed_recv.at[turn, k], hub + i, place
        )

    def feed_wait(turn, k):
        part = m_all.at[turn, k]
        remote(
            part, part, pass_send.at[0, 0], feed_recv.at[turn, k], partner, place
        ).wait_recv()

    def pass_on(turn, k):
        return remote(
            m_all.at[turn, k], m_all.at[turn, k + 1], pass_send.at[turn, k],
            feed_recv.at[turn, k + 1], site, at(-1),
        )

    def pass_first(turn):
        return remote(
            ring.at[0, parity], m_all.at[turn, 1], pass_send.at[turn, 0],
            feed_recv.at[turn, 1], site, at(-1),
        )

    def start(blocks, target, slot):
        low = blocks[0]
        mid = blocks[1:3].reshape(2 * width, width)
        top = blocks[3]
        step = 32
        for row in range(0, width, step):
            g0 = nt(low[row : row + step], low)
            g1 = nt(mid[row : row + step], mid)
            g2 = nt(mid[width + row : width + row + step], mid)
            g3 = nt(top[row : row + step], top)
            parts = (g0, g1[:, :width], g1[:, width:], g2[:, :width], g2[:, width:], g3)
            parts = [x.reshape(step // 8, 8, width) for x in parts]
            for w in range(channels):
                block = parts[0] * coef[0, w][None]
                for i in range(1, len(PAIRS)):
                    block = block + parts[i] * coef[i, w][None]
                target[w, row : row + step, :] = block.reshape(step, width).astype(BF16)

        @pl.when(slot == 0)
        def _():
            small = target[...].astype(F32).reshape(channels * width // 8, 8, width) * SMALL
            squares[0, 0] += jnp.sum(small * small, axis=0)

    def swap_part(turn, j, part):
        last = turn == SITES - 1
        arrival = jnp.where(last, parity, j)
        return remote(
            part, part, swap_send.at[turn, j], swap_recv.at[turn, arrival],
            jnp.where(last, end, partner), place,
        )

    def swap(turn, j):
        return swap_part(turn, j, r_all.at[turn, parity, j])

    def swap_pair(turn, j, pair):
        @pl.when(swaps(turn, j))
        def _():
            swap_part(turn, j, r_all.at[turn, parity, j, pl.ds(2 * pair, 2)]).start()

    def advance(turn, j):
        prev = turn - 1
        low = m_all[turn, j, 0]
        mid = m_all[turn, j, 1:3].reshape(2 * width, width)
        top = m_all[turn, j, 3]
        step = 32

        one = channels * 8

        def keep(row, first, x):
            y = x.reshape(channels, step // 8, 8, width)
            for i in range(step // 16):
                cut = [y[:, 2 * i + h].reshape(one, width) for h in range(2)]
                both = jnp.concatenate(cut, axis=1).astype(BF16)
                inner[row // 16 + i, first : first + one] = both

        for row in range(0, width, step):
            def rows_of(which, slot):
                rows = r_all[prev, which, slot, :, row : row + step, :]
                return rows.reshape(channels * step, width)

            keep(row, 0, nt(rows_of(parity, j), low))
            x = nt(rows_of(1 - parity, j + parity), mid)
            keep(row, one, x[:, :width])
            keep(row, 2 * one, x[:, width:])
            keep(row, 3 * one, nt(rows_of(parity, j + 1), top))

        def put(s, i, y):
            z = y.reshape(channels, 8, 2 * width)
            at_row = s * width + 16 * i
            for w in range(channels):
                both = jnp.concatenate([z[w, :, :width], z[w, :, width:]], axis=0)
                lane = (w % 2) * width
                mixed[w // 2, at_row : at_row + 16, lane : lane + width] = both.astype(BF16)

        for i in range(width // 16):
            put(0, i, nn(mix_low[prev], inner[i, :one]))
        for i in range(width // 16):
            y = nn(mix_mid[prev], inner[i, one : 3 * one])
            put(1, i, y[:one])
            put(2, i, y[one:])
        for i in range(width // 16):
            put(3, i, nn(mix_top[prev], inner[i, 3 * one :]))
        wide = jnp.concatenate([low, mid[:width], mid[width:], top], axis=1)
        total = jnp.zeros((8, 2 * width), F32)
        for pair in range(channels // 2):
            block = nn(wide, mixed[pair])
            r_all[turn, parity, j, 2 * pair] = block[:, :width].astype(BF16)
            r_all[turn, parity, j, 2 * pair + 1] = block[:, width:].astype(BF16)
            small = block * SMALL
            total = total + jnp.sum((small * small).reshape(width // 8, 8, 2 * width), axis=0)
            if pair > 0:
                swap_pair(turn, j, pair - 1)
        slot = (j >= 1).astype(jnp.int32)
        squares[slot, turn] += total[:, :width] + total[:, width:]
        swap_pair(turn, j, channels // 2 - 1)

    def swap_wait(turn, j):
        part = r_all.at[turn, 1 - parity, j]
        remote(
            part, part, swap_send.at[turn, j], swap_recv.at[turn, j], partner, place
        ).wait_recv()

    def swaps(turn, j):
        even = (parity == 0) & ((j >= 1) | (turn == 1))
        odd = (parity == 1) & (j <= 2 - turn)
        return (turn == 3) | even | odd

    def tell(i):
        for step in (ROUNDS[i], -ROUNDS[i]):
            pl.semaphore_signal(
                round_sem.at[i], inc=1, device_id=(site, at(step)), device_id_type=MESH
            )

    def told(i):
        pl.semaphore_wait(round_sem.at[i], 2)

    targets = (end, hub, hub + 1, far)

    def sum_copy(kind, step):
        return remote(
            mine, heard.at[parity * places + place], sum_send.at[kind, step], sum_recv,
            targets[kind], at(step),
        )

    def sum_self(kind, step):
        return (step == 0) & (kind == parity + 1)

    @pl.when(role == 2)
    def _():
        pl.semaphore_wait(barrier, 4)

        @pl.loop(0, REACH)
        def _(k):
            for i in range(held):
                for h in range(2):
                    @pl.when(k > 0)
                    def _():
                        ring_wait(k, i, h)

                    @pl.when(k < REACH - 1)
                    def _():
                        ring_copy(k, i, h).start()

                    feed_half(k, i, h).start()

        load_weights()
        edge_of(table_of(SITES - 1, mpo_ref, mask_ref, table), channels, coef)
        squares[...] = jnp.zeros_like(squares)

        @pl.loop(0, held)
        def _(i):
            start(ring.at[0, i], r_all.at[0, i, 0], 1)

    @pl.when(role == 3)
    def _():
        pl.semaphore_wait(barrier, 2)
        for i in range(held):
            feed(3, 0, i, ring.at[0, i], feed_send.at[0, i]).start()
        load_weights()

    @pl.when(works)
    def _():
        home = 2 - parity
        pl.semaphore_wait(barrier, 5)
        tell(0)
        feed(home, 0, 1 - parity, ring.at[0, 1 - parity], feed_send.at[0, 0]).start()
        pass_first(home).start()
        m_all[home, 0] = ring[0, parity]
        load_weights()
        edge_of(table_of(SITES - 1, mpo_ref, mask_ref, table), channels, coef)
        squares[...] = jnp.zeros_like(squares)
        feed_wait(1 + parity, 0)
        pass_on(1 + parity, 0).start()
        told(0)
        tell(1)
        for turn in range(1, SITES):
            found = table_of(SITES - 1 - turn, mpo_ref, mask_ref, table)
            mix_low[turn - 1] = spread(found, channels, 0, 1)
            mix_mid[turn - 1] = spread(found, channels, 1, 2)
            mix_top[turn - 1] = spread(found, channels, 3, 1)
        feed_wait(1, 1)
        pass_on(1, 1).start()
        told(1)
        tell(2)

        @pl.loop(0, REACH)
        def _(k):
            feed_wait(0, k)
            start(m_all.at[0, k], r_all.at[0, parity, k], (k >= 1).astype(jnp.int32))

            @pl.when(swaps(0, k))
            def _():
                swap(0, k).start()

            @pl.loop(1, k + 1)
            def _(t):
                @pl.when(k == REACH - 1)
                def _():
                    feed_wait(t, k - t)

                swap_wait(t - 1, k - t + parity)
                advance(t, k - t)

            @pl.when(k == 1)
            def _():
                told(2)
                tell(3)

        lane = ids(1, width, 1)
        row = jnp.zeros((1, width), F32)
        for t in range(SITES):
            row = row + jnp.where(lane == t, jnp.sum(squares[0, t]), 0.0)
        mine[...] = row
        heard[parity * places + place] = row
        told(3)

        for kind in range(4):
            @pl.loop(0, places)
            def _(step):
                @pl.when(jnp.logical_not(sum_self(kind, step)))
                def _():
                    sum_copy(kind, step).start()

    def heard_all(count):
        part = heard.at[pl.ds(0, count)]
        remote(part, part, sum_send.at[0, 0], sum_recv, site, at(1)).wait_recv()

    @pl.when(role == 3)
    def _():
        for i in range(held):
            part = r_all.at[3, i, 0]
            remote(
                part, part, swap_send.at[3, 0], swap_recv.at[3, i], hub + i, place
            ).wait_recv()

    @pl.when(role == 1)
    def _():
        swap_wait(1, 0)

    @pl.when(works)
    def _():
        heard_all(2 * places - 1)

    @pl.when(role >= 2)
    def _():
        heard_all(2 * places)

    turn = jnp.where(role == 3, 3, 2 - role)
    sums = jnp.sum(heard[...].reshape(2 * places, width), axis=0, keepdims=True)
    entries = float(places * held * channels * width * width)
    unit = jnp.ones((1, 1), F32)
    chosen = unit
    for t in range(SITES):
        square = sums[:, t : t + 1] * (1.0 / (SMALL * SMALL * entries)) * unit * unit
        unit = unit * lax.rsqrt(square + EPSILON)
        chosen = jnp.where(turn == t, unit, chosen)
    scale_ref[...] = jnp.broadcast_to(chosen, scale_ref.shape)
    for i in range(held):
        out_ref[i] = r_all[turn, i, 0]

    @pl.when(works)
    def _():
        home = 2 - parity
        feed(home, 0, 1 - parity, ring.at[0, 1 - parity], feed_send.at[0, 0]).wait_send()
        for t, k in ((1, 0), (1, 1), (2, 0)):
            pass_on(t, k).wait_send()
        for t in range(SITES):
            for j in range(REACH - t):
                @pl.when(swaps(t, j))
                def _():
                    swap(t, j).wait_send()
        for kind in range(4):
            @pl.loop(0, places)
            def _(step):
                @pl.when(jnp.logical_not(sum_self(kind, step)))
                def _():
                    sum_copy(kind, step).wait_send()

    @pl.when(role == 2)
    def _():
        for k in range(REACH):
            for i in range(held):
                for h in range(2):
                    if k < REACH - 1:
                        ring_copy(k, i, h).wait_send()
                feed(0, k, i, ring.at[k, i], feed_send.at[k, i]).wait_send()

    @pl.when(role == 3)
    def _():
        for i in range(held):
            feed(3, 0, i, ring.at[0, i], feed_send.at[0, i]).wait_send()


def scaled(in_ref, scale_ref, out_ref, final, done_sem):
    channels = final.shape[1]
    factor = scale_ref[0:1, :].reshape(1, 1, final.shape[-1])

    def put(w):
        return pltpu.make_async_copy(final.at[:, w], out_ref.at[:, w], done_sem.at[w])

    for w in range(channels):
        final[:, w] = (in_ref[:, w].astype(F32) * factor).astype(BF16)
        put(w).start()
    for w in range(channels):
        put(w).wait()


def on_device(mps, mpo, mpo_mask, sector_size, pair_live):
    places = lax.axis_size("tensor")
    held, width = mps.shape[1], mps.shape[-1]
    channels = mpo.shape[1]
    vmem, dma = pltpu.VMEM, pltpu.SemaphoreType.DMA
    in_vmem, in_hbm = pl.BlockSpec(memory_space=pltpu.VMEM), pl.BlockSpec(memory_space=pltpu.HBM)
    result = (held, channels, width, width)
    environment, scale = pl.pallas_call(
        kernel,
        out_shape=(
            jax.ShapeDtypeStruct(result, BF16),
            jax.ShapeDtypeStruct((8, width), F32),
        ),
        in_specs=[in_hbm] * 5,
        out_specs=(in_vmem, in_vmem),
        scratch_shapes=[
            vmem((SITES, channels, PHYS, PHYS, channels), BF16),
            vmem((channels, SITES, channels), jnp.int32),
            pltpu.SMEM((1, held), jnp.int32),
            pltpu.SMEM((1, held, 3), jnp.int32),
            vmem((held, PHYS, width, width), BF16),
            vmem((REACH, held, PHYS, width, width), BF16),
            vmem((SITES, REACH, PHYS, width, width), BF16),
            vmem((SITES, 2, REACH, channels, width, width), BF16),
            vmem((SITES - 1, channels * 8, channels * 8), BF16),
            vmem((SITES - 1, channels * 16, channels * 16), BF16),
            vmem((SITES - 1, channels * 8, channels * 8), BF16),
            vmem((len(PAIRS), channels, 8, width), F32),
            vmem((channels * PHYS * PHYS, width), F32),
            vmem((width // 16, PHYS * channels * 8, 2 * width), BF16),
            vmem((channels // 2, PHYS * width, 2 * width), BF16),
            vmem((2, SITES, 8, width), F32),
            vmem((1, width), F32),
            vmem((2 * places, 1, width), F32),
            dma((5,)),
            dma((REACH, held, 2)),
            dma((REACH, held, 2)),
            dma((REACH, held)),
            dma((SITES, REACH)),
            dma((SITES, REACH)),
            dma((SITES, REACH)),
            dma((SITES, REACH)),
            dma((SITES, places)),
            dma,
            pltpu.SemaphoreType.REGULAR((len(ROUNDS),)),
        ],
        compiler_params=pltpu.CompilerParams(
            collective_id=0, has_side_effects=True, vmem_limit_bytes=48 * 1024 * 1024
        ),
    )(
        *[
            pltpu.with_memory_space_constraint(x, pltpu.HBM)
            for x in (
                mps[0],
                jnp.transpose(mpo, (0, 1, 3, 4, 2)),
                jnp.transpose(mpo_mask, (1, 0, 2)),
                sector_size,
                pair_live,
            )
        ]
    )
    return pl.pallas_call(
        scaled,
        out_shape=jax.ShapeDtypeStruct(result, BF16),
        in_specs=[in_vmem, in_vmem],
        out_specs=pl.BlockSpec(memory_space=pl.ANY),
        scratch_shapes=[vmem(result, BF16), dma((channels,))],
        compiler_params=pltpu.CompilerParams(vmem_limit_bytes=4 * 1024 * 1024),
    )(environment, scale)[None]


def solution(mesh):
    in_specs = (
        P("site", "tensor", None, None, None),
        P(),
        P(),
        P("site", "tensor"),
        P("site", "tensor", None),
    )
    out_specs = P("site", "tensor", None, None, None)
    return jax.shard_map(
        on_device, mesh=mesh, in_specs=in_specs, out_specs=out_specs, check_vma=False
    )
```

```python
import jax
import jax.numpy as jnp
from jax import lax
from jax.experimental import pallas as pl
from jax.experimental.pallas import tpu as pltpu
from jax.sharding import PartitionSpec as P

SITES = 4
PHYS = 4
CHARGE = (0, 1, 1, 2)
PAIRS = (0, 5, 6, 9, 10, 15)
ROUNDS = (1, 2, 4, 1)
MESH = pl.DeviceIdType.MESH
EPSILON = 1e-06
SMALL = 2.0**-12
F32 = jnp.float32
BF16 = jnp.bfloat16
REACH = 4


def nt(a, b):
    return lax.dot_general(a, b, (((1,), (1,)), ((), ())), preferred_element_type=F32)


def nn(a, b):
    return lax.dot_general(a, b, (((1,), (0,)), ((), ())), preferred_element_type=F32)


def ids(rows, columns, axis):
    return lax.broadcasted_iota(jnp.int32, (rows, columns), axis)


def table_of(p, mpo_ref, mask_ref, table):
    channels = mask_ref.shape[0]
    table[...] = jnp.zeros_like(table)
    for w in range(channels):
        keep = mask_ref[w, p : p + 1, :] > 0
        for s in range(PHYS):
            tile = jnp.where(keep, mpo_ref[p, w, s].astype(F32), 0.0)
            at = (w * PHYS + s) * PHYS
            table[at : at + PHYS, :channels] = tile
    return table[...].astype(BF16)


def one_hot(condition):
    return jnp.where(condition, 1.0, 0.0).astype(BF16)


def spread(table, channels, first, count):
    one = channels * 8
    size, depth = count * one, table.shape[0]

    def split(x):
        state = jnp.where(x >= one, 1, 0)
        return state + first, (x - state * one) // 8

    _, channel_of_column = split(ids(table.shape[1], size, 1))
    wide = nn(table, one_hot(ids(table.shape[1], size, 0) == channel_of_column))
    state_of_column, _ = split(ids(depth, size, 1))
    wide = jnp.where(ids(depth, size, 0) % PHYS == state_of_column, wide, 0.0).astype(BF16)
    state_of_row, channel_of_row = split(ids(size, depth, 0))
    entry = ids(size, depth, 1)
    pick = one_hot(entry // PHYS == channel_of_row * PHYS + state_of_row)
    full = nn(pick, wide)
    return jnp.where(ids(size, size, 0) % 8 == ids(size, size, 1) % 8, full, 0.0).astype(BF16)


def edge_of(table, channels, coef):
    depth, lanes = table.shape
    last = nn(table, one_hot(ids(lanes, lanes, 0) == channels - 1)).astype(BF16)
    rows = channels * 8
    for i, code in enumerate(PAIRS):
        pick = one_hot(ids(rows, depth, 1) == ids(rows, depth, 0) // 8 * PHYS * PHYS + code)
        coef[i] = nn(pick, last).reshape(channels, 8, lanes)


def kernel(
    m_ref, mpo_in, mask_in, size_in, live_in, out_ref, scale_ref,
    mpo_ref, mask_ref, size_ref, live_ref, raw, ring, m_all, r_all, mix_low, mix_mid, mix_top, coef, table, inner, mixed, squares, mine, heard,
    load_sem, ring_send, ring_recv, feed_send, feed_recv, pass_send, swap_send, swap_recv,
    sum_send, sum_recv, round_sem,
):
    site, place = lax.axis_index("site"), lax.axis_index("tensor")
    sites, places = lax.axis_size("site"), lax.axis_size("tensor")
    role = site % SITES
    hub = jnp.where(role == 3, (site + 1) % sites, site - role)
    channels, width = r_all.shape[3], r_all.shape[4]
    held = m_ref.shape[0]
    far = hub + 2
    end = (hub + sites - 1) % sites
    parity = jnp.where(role == 1, 1, 0)
    partner = hub + 1 - parity
    works = role < 2

    def at(step):
        return lax.rem(place + step + places, places)

    loads = [
        pltpu.make_async_copy(src, dst, load_sem.at[i])
        for i, (src, dst) in enumerate((
            (m_ref, raw), (size_in, size_ref), (live_in, live_ref),
            (mpo_in, mpo_ref), (mask_in, mask_ref),
        ))
    ]
    for load in loads:
        load.start()
    barrier = pltpu.get_barrier_semaphore()

    def greet(*targets):
        for site_to, place_to in targets:
            pl.semaphore_signal(barrier, inc=1, device_id=(site_to, place_to), device_id_type=MESH)

    @pl.when(works)
    def _():
        greet((far, place), (end, place), (partner, place), (site, at(1)), (site, at(-1)))

    @pl.when(role == 2)
    def _():
        greet((hub, place), (hub + 1, place), (site, at(1)), (site, at(-1)))

    @pl.when(role == 3)
    def _():
        greet((hub, place), (hub + 1, place))

    for load in loads[:3]:
        load.wait()
    for i in range(held):
        sector = place * held + i
        for s in range(PHYS):
            charge = CHARGE[s]
            live = (live_ref[0, i, charge] > 0) & (sector + charge < places * held)
            bound = jnp.where(live, size_ref[0, i], 0)
            block = jnp.where(ids(width, width, 0) < bound, raw[i, s].astype(F32), 0.0)
            ring[0, i, s] = block.astype(BF16)

    def load_weights():
        for load in loads[3:]:
            load.wait()

    def remote(src, dst, send, recv, site_to, place_to):
        return pltpu.make_async_remote_copy(
            src_ref=src, dst_ref=dst, send_sem=send, recv_sem=recv,
            device_id=(site_to, place_to), device_id_type=MESH,
        )

    def half(k, i, h):
        return ring.at[k, i, pl.ds(2 * h, 2)]

    def ring_copy(k, i, h):
        return remote(
            half(k, i, h), half(k + 1, i, h), ring_send.at[k, i, h], ring_recv.at[k + 1, i, h],
            site, at(-1),
        )

    def ring_wait(k, i, h):
        remote(
            half(k, i, h), half(k, i, h), ring_send.at[0, 0, 0], ring_recv.at[k, i, h],
            site, at(-1),
        ).wait_recv()

    def feed_half(k, i, h):
        return remote(
            half(k, i, h), m_all.at[0, k, pl.ds(2 * h, 2)], feed_send.at[k, i],
            feed_recv.at[0, k], hub + i, place,
        )

    def feed(turn, k, i, source, send):
        return remote(
            source, m_all.at[turn, k], send, feed_recv.at[turn, k], hub + i, place
        )

    def feed_wait(turn, k):
        part = m_all.at[turn, k]
        remote(
            part, part, pass_send.at[0, 0], feed_recv.at[turn, k], partner, place
        ).wait_recv()

    def pass_on(turn, k):
        return remote(
            m_all.at[turn, k], m_all.at[turn, k + 1], pass_send.at[turn, k],
            feed_recv.at[turn, k + 1], site, at(-1),
        )

    def pass_first(turn):
        return remote(
            ring.at[0, parity], m_all.at[turn, 1], pass_send.at[turn, 0],
            feed_recv.at[turn, 1], site, at(-1),
        )

    def start(blocks, target, slot):
        low = blocks[0]
        mid = blocks[1:3].reshape(2 * width, width)
        top = blocks[3]
        step = 32
        for row in range(0, width, step):
            g0 = nt(low[row : row + step], low)
            g1 = nt(mid[row : row + step], mid)
            g2 = nt(mid[width + row : width + row + step], mid)
            g3 = nt(top[row : row + step], top)
            parts = (g0, g1[:, :width], g1[:, width:], g2[:, :width], g2[:, width:], g3)
            parts = [x.reshape(step // 8, 8, width) for x in parts]
            for w in range(channels):
                block = parts[0] * coef[0, w][None]
                for i in range(1, len(PAIRS)):
                    block = block + parts[i] * coef[i, w][None]
                target[w, row : row + step, :] = block.reshape(step, width).astype(BF16)

        @pl.when(slot == 0)
        def _():
            small = target[...].astype(F32).reshape(channels * width // 8, 8, width) * SMALL
            squares[0, 0] += jnp.sum(small * small, axis=0)

    def swap_part(turn, j, part):
        last = turn == SITES - 1
        arrival = jnp.where(last, parity, j)
        return remote(
            part, part, swap_send.at[turn, j], swap_recv.at[turn, arrival],
            jnp.where(last, end, partner), place,
        )

    def swap(turn, j):
        return swap_part(turn, j, r_all.at[turn, parity, j])

    def swap_pair(turn, j, pair):
        @pl.when(swaps(turn, j))
        def _():
            swap_part(turn, j, r_all.at[turn, parity, j, pl.ds(2 * pair, 2)]).start()

    def advance(turn, j):
        prev = turn - 1
        low = m_all[turn, j, 0]
        mid = m_all[turn, j, 1:3].reshape(2 * width, width)
        top = m_all[turn, j, 3]
        step = 32

        one = channels * 8

        def keep(row, first, x):
            y = x.reshape(channels, step // 8, 8, width)
            for i in range(step // 16):
                cut = [y[:, 2 * i + h].reshape(one, width) for h in range(2)]
                both = jnp.concatenate(cut, axis=1).astype(BF16)
                inner[row // 16 + i, first : first + one] = both

        for row in range(0, width, step):
            def rows_of(which, slot):
                rows = r_all[prev, which, slot, :, row : row + step, :]
                return rows.reshape(channels * step, width)

            keep(row, 0, nt(rows_of(parity, j), low))
            x = nt(rows_of(1 - parity, j + parity), mid)
            keep(row, one, x[:, :width])
            keep(row, 2 * one, x[:, width:])
            keep(row, 3 * one, nt(rows_of(parity, j + 1), top))

        def put(s, i, y):
            z = y.reshape(channels, 8, 2 * width)
            at_row = s * width + 16 * i
            for w in range(channels):
                both = jnp.concatenate([z[w, :, :width], z[w, :, width:]], axis=0)
                lane = (w % 2) * width
                mixed[w // 2, at_row : at_row + 16, lane : lane + width] = both.astype(BF16)

        for i in range(width // 16):
            put(0, i, nn(mix_low[prev], inner[i, :one]))
        for i in range(width // 16):
            y = nn(mix_mid[prev], inner[i, one : 3 * one])
            put(1, i, y[:one])
            put(2, i, y[one:])
        for i in range(width // 16):
            put(3, i, nn(mix_top[prev], inner[i, 3 * one :]))
        wide = jnp.concatenate([low, mid[:width], mid[width:], top], axis=1)
        total = jnp.zeros((8, 2 * width), F32)
        for pair in range(channels // 2):
            block = nn(wide, mixed[pair])
            r_all[turn, parity, j, 2 * pair] = block[:, :width].astype(BF16)
            r_all[turn, parity, j, 2 * pair + 1] = block[:, width:].astype(BF16)
            small = block * SMALL
            total = total + jnp.sum((small * small).reshape(width // 8, 8, 2 * width), axis=0)
        slot = (j >= 1).astype(jnp.int32)
        squares[slot, turn] += total[:, :width] + total[:, width:]

        @pl.when(swaps(turn, j))
        def _():
            swap(turn, j).start()

    def swap_wait(turn, j):
        part = r_all.at[turn, 1 - parity, j]
        remote(
            part, part, swap_send.at[turn, j], swap_recv.at[turn, j], partner, place
        ).wait_recv()

    def swaps(turn, j):
        even = (parity == 0) & ((j >= 1) | (turn == 1))
        odd = (parity == 1) & (j <= 2 - turn)
        return (turn == 3) | even | odd

    def tell(i):
        for step in (ROUNDS[i], -ROUNDS[i]):
            pl.semaphore_signal(
                round_sem.at[i], inc=1, device_id=(site, at(step)), device_id_type=MESH
            )

    def told(i):
        pl.semaphore_wait(round_sem.at[i], 2)

    targets = (end, hub, hub + 1, far)

    def sum_copy(kind, step):
        return remote(
            mine, heard.at[parity * places + place], sum_send.at[kind, step], sum_recv,
            targets[kind], at(step),
        )

    def sum_self(kind, step):
        return (step == 0) & (kind == parity + 1)

    @pl.when(role == 2)
    def _():
        pl.semaphore_wait(barrier, 4)

        @pl.loop(0, REACH)
        def _(k):
            for i in range(held):
                for h in range(2):
                    @pl.when(k > 0)
                    def _():
                        ring_wait(k, i, h)

                    @pl.when(k < REACH - 1)
                    def _():
                        ring_copy(k, i, h).start()

                    feed_half(k, i, h).start()

        load_weights()
        edge_of(table_of(SITES - 1, mpo_ref, mask_ref, table), channels, coef)
        squares[...] = jnp.zeros_like(squares)

        @pl.loop(0, held)
        def _(i):
            start(ring.at[0, i], r_all.at[0, i, 0], 1)

    @pl.when(role == 3)
    def _():
        pl.semaphore_wait(barrier, 2)
        for i in range(held):
            feed(3, 0, i, ring.at[0, i], feed_send.at[0, i]).start()
        load_weights()

    @pl.when(works)
    def _():
        home = 2 - parity
        pl.semaphore_wait(barrier, 5)
        tell(0)
        feed(home, 0, 1 - parity, ring.at[0, 1 - parity], feed_send.at[0, 0]).start()
        pass_first(home).start()
        m_all[home, 0] = ring[0, parity]
        load_weights()
        edge_of(table_of(SITES - 1, mpo_ref, mask_ref, table), channels, coef)
        squares[...] = jnp.zeros_like(squares)
        feed_wait(1 + parity, 0)
        pass_on(1 + parity, 0).start()
        told(0)
        tell(1)
        for turn in range(1, SITES):
            found = table_of(SITES - 1 - turn, mpo_ref, mask_ref, table)
            mix_low[turn - 1] = spread(found, channels, 0, 1)
            mix_mid[turn - 1] = spread(found, channels, 1, 2)
            mix_top[turn - 1] = spread(found, channels, 3, 1)

        @pl.loop(0, REACH)
        def _(k):
            feed_wait(0, k)
            start(m_all.at[0, k], r_all.at[0, parity, k], (k >= 1).astype(jnp.int32))

            @pl.when(swaps(0, k))
            def _():
                swap(0, k).start()

            @pl.loop(1, k + 1)
            def _(t):
                @pl.when(k == REACH - 1)
                def _():
                    feed_wait(t, k - t)

                swap_wait(t - 1, k - t + parity)
                advance(t, k - t)

            @pl.when(k == 0)
            def _():
                feed_wait(1, 1)
                pass_on(1, 1).start()
                told(1)
                tell(2)

            @pl.when(k == 1)
            def _():
                told(2)
                tell(3)

        lane = ids(1, width, 1)
        row = jnp.zeros((1, width), F32)
        for t in range(SITES):
            row = row + jnp.where(lane == t, jnp.sum(squares[0, t]), 0.0)
        mine[...] = row
        heard[parity * places + place] = row
        told(3)

        for kind in range(4):
            @pl.loop(0, places)
            def _(step):
                @pl.when(jnp.logical_not(sum_self(kind, step)))
                def _():
                    sum_copy(kind, step).start()

    def heard_all(count):
        part = heard.at[pl.ds(0, count)]
        remote(part, part, sum_send.at[0, 0], sum_recv, site, at(1)).wait_recv()

    @pl.when(role == 3)
    def _():
        for i in range(held):
            part = r_all.at[3, i, 0]
            remote(
                part, part, swap_send.at[3, 0], swap_recv.at[3, i], hub + i, place
            ).wait_recv()

    @pl.when(role == 1)
    def _():
        swap_wait(1, 0)

    @pl.when(works)
    def _():
        heard_all(2 * places - 1)

    @pl.when(role >= 2)
    def _():
        heard_all(2 * places)

    turn = jnp.where(role == 3, 3, 2 - role)
    sums = jnp.sum(heard[...].reshape(2 * places, width), axis=0, keepdims=True)
    entries = float(places * held * channels * width * width)
    unit = jnp.ones((1, 1), F32)
    chosen = unit
    for t in range(SITES):
        square = sums[:, t : t + 1] * (1.0 / (SMALL * SMALL * entries)) * unit * unit
        unit = unit * lax.rsqrt(square + EPSILON)
        chosen = jnp.where(turn == t, unit, chosen)
    scale_ref[...] = jnp.broadcast_to(chosen, scale_ref.shape)
    for i in range(held):
        out_ref[i] = r_all[turn, i, 0]

    @pl.when(works)
    def _():
        home = 2 - parity
        feed(home, 0, 1 - parity, ring.at[0, 1 - parity], feed_send.at[0, 0]).wait_send()
        for t, k in ((1, 0), (1, 1), (2, 0)):
            pass_on(t, k).wait_send()
        for t in range(SITES):
            for j in range(REACH - t):
                @pl.when(swaps(t, j))
                def _():
                    swap(t, j).wait_send()
        for kind in range(4):
            @pl.loop(0, places)
            def _(step):
                @pl.when(jnp.logical_not(sum_self(kind, step)))
                def _():
                    sum_copy(kind, step).wait_send()

    @pl.when(role == 2)
    def _():
        for k in range(REACH):
            for i in range(held):
                for h in range(2):
                    if k < REACH - 1:
                        ring_copy(k, i, h).wait_send()
                feed(0, k, i, ring.at[k, i], feed_send.at[k, i]).wait_send()

    @pl.when(role == 3)
    def _():
        for i in range(held):
            feed(3, 0, i, ring.at[0, i], feed_send.at[0, i]).wait_send()


def scaled(in_ref, scale_ref, out_ref, final, done_sem):
    channels = final.shape[1]
    factor = scale_ref[0:1, :].reshape(1, 1, final.shape[-1])

    def put(w):
        return pltpu.make_async_copy(final.at[:, w], out_ref.at[:, w], done_sem.at[w])

    for w in range(channels):
        final[:, w] = (in_ref[:, w].astype(F32) * factor).astype(BF16)
        put(w).start()
    for w in range(channels):
        put(w).wait()


def on_device(mps, mpo, mpo_mask, sector_size, pair_live):
    places = lax.axis_size("tensor")
    held, width = mps.shape[1], mps.shape[-1]
    channels = mpo.shape[1]
    vmem, dma = pltpu.VMEM, pltpu.SemaphoreType.DMA
    in_vmem, in_hbm = pl.BlockSpec(memory_space=pltpu.VMEM), pl.BlockSpec(memory_space=pltpu.HBM)
    result = (held, channels, width, width)
    environment, scale = pl.pallas_call(
        kernel,
        out_shape=(
            jax.ShapeDtypeStruct(result, BF16),
            jax.ShapeDtypeStruct((8, width), F32),
        ),
        in_specs=[in_hbm] * 5,
        out_specs=(in_vmem, in_vmem),
        scratch_shapes=[
            vmem((SITES, channels, PHYS, PHYS, channels), BF16),
            vmem((channels, SITES, channels), jnp.int32),
            pltpu.SMEM((1, held), jnp.int32),
            pltpu.SMEM((1, held, 3), jnp.int32),
            vmem((held, PHYS, width, width), BF16),
            vmem((REACH, held, PHYS, width, width), BF16),
            vmem((SITES, REACH, PHYS, width, width), BF16),
            vmem((SITES, 2, REACH, channels, width, width), BF16),
            vmem((SITES - 1, channels * 8, channels * 8), BF16),
            vmem((SITES - 1, channels * 16, channels * 16), BF16),
            vmem((SITES - 1, channels * 8, channels * 8), BF16),
            vmem((len(PAIRS), channels, 8, width), F32),
            vmem((channels * PHYS * PHYS, width), F32),
            vmem((width // 16, PHYS * channels * 8, 2 * width), BF16),
            vmem((channels // 2, PHYS * width, 2 * width), BF16),
            vmem((2, SITES, 8, width), F32),
            vmem((1, width), F32),
            vmem((2 * places, 1, width), F32),
            dma((5,)),
            dma((REACH, held, 2)),
            dma((REACH, held, 2)),
            dma((REACH, held)),
            dma((SITES, REACH)),
            dma((SITES, REACH)),
            dma((SITES, REACH)),
            dma((SITES, REACH)),
            dma((SITES, places)),
            dma,
            pltpu.SemaphoreType.REGULAR((len(ROUNDS),)),
        ],
        compiler_params=pltpu.CompilerParams(
            collective_id=0, has_side_effects=True, vmem_limit_bytes=48 * 1024 * 1024
        ),
    )(
        *[
            pltpu.with_memory_space_constraint(x, pltpu.HBM)
            for x in (
                mps[0],
                jnp.transpose(mpo, (0, 1, 3, 4, 2)),
                jnp.transpose(mpo_mask, (1, 0, 2)),
                sector_size,
                pair_live,
            )
        ]
    )
    return pl.pallas_call(
        scaled,
        out_shape=jax.ShapeDtypeStruct(result, BF16),
        in_specs=[in_vmem, in_vmem],
        out_specs=pl.BlockSpec(memory_space=pl.ANY),
        scratch_shapes=[vmem(result, BF16), dma((channels,))],
        compiler_params=pltpu.CompilerParams(vmem_limit_bytes=4 * 1024 * 1024),
    )(environment, scale)[None]


def solution(mesh):
    in_specs = (
        P("site", "tensor", None, None, None),
        P(),
        P(),
        P("site", "tensor"),
        P("site", "tensor", None),
    )
    out_specs = P("site", "tensor", None, None, None)
    return jax.shard_map(
        on_device, mesh=mesh, in_specs=in_specs, out_specs=out_specs, check_vma=False
    )
```

```python
import jax
import jax.numpy as jnp
from jax import lax
from jax.experimental import pallas as pl
from jax.experimental.pallas import tpu as pltpu
from jax.sharding import PartitionSpec as P

SITES = 4
PHYS = 4
CHARGE = (0, 1, 1, 2)
PAIRS = (0, 5, 6, 9, 10, 15)
ROUNDS = (1, 2, 4, 1)
MESH = pl.DeviceIdType.MESH
EPSILON = 1e-06
SMALL = 2.0**-12
F32 = jnp.float32
BF16 = jnp.bfloat16
REACH = 4


def nt(a, b):
    return lax.dot_general(a, b, (((1,), (1,)), ((), ())), preferred_element_type=F32)


def nn(a, b):
    return lax.dot_general(a, b, (((1,), (0,)), ((), ())), preferred_element_type=F32)


def ids(rows, columns, axis):
    return lax.broadcasted_iota(jnp.int32, (rows, columns), axis)


def table_of(p, mpo_ref, mask_ref, table):
    channels = mask_ref.shape[0]
    table[...] = jnp.zeros_like(table)
    for w in range(channels):
        keep = mask_ref[w, p : p + 1, :] > 0
        for s in range(PHYS):
            tile = jnp.where(keep, mpo_ref[p, w, s].astype(F32), 0.0)
            at = (w * PHYS + s) * PHYS
            table[at : at + PHYS, :channels] = tile
    return table[...].astype(BF16)


def one_hot(condition):
    return jnp.where(condition, 1.0, 0.0).astype(BF16)


def spread(table, channels, first, count):
    one = channels * 8
    size, depth = count * one, table.shape[0]

    def split(x):
        state = jnp.where(x >= one, 1, 0)
        return state + first, (x - state * one) // 8

    _, channel_of_column = split(ids(table.shape[1], size, 1))
    wide = nn(table, one_hot(ids(table.shape[1], size, 0) == channel_of_column))
    state_of_column, _ = split(ids(depth, size, 1))
    wide = jnp.where(ids(depth, size, 0) % PHYS == state_of_column, wide, 0.0).astype(BF16)
    state_of_row, channel_of_row = split(ids(size, depth, 0))
    entry = ids(size, depth, 1)
    pick = one_hot(entry // PHYS == channel_of_row * PHYS + state_of_row)
    full = nn(pick, wide)
    return jnp.where(ids(size, size, 0) % 8 == ids(size, size, 1) % 8, full, 0.0).astype(BF16)


def edge_of(table, channels, coef):
    depth, lanes = table.shape
    last = nn(table, one_hot(ids(lanes, lanes, 0) == channels - 1)).astype(BF16)
    rows = channels * 8
    for i, code in enumerate(PAIRS):
        pick = one_hot(ids(rows, depth, 1) == ids(rows, depth, 0) // 8 * PHYS * PHYS + code)
        coef[i] = nn(pick, last).reshape(channels, 8, lanes)


def kernel(
    m_ref, mpo_in, mask_in, size_in, live_in, out_ref, scale_ref,
    mpo_ref, mask_ref, size_ref, live_ref, raw, ring, m_all, r_all, mix_low, mix_mid, mix_top, coef, table, inner, mixed, squares, mine, heard,
    load_sem, ring_send, ring_recv, feed_send, feed_recv, pass_send, swap_send, swap_recv,
    sum_send, sum_recv, round_sem,
):
    site, place = lax.axis_index("site"), lax.axis_index("tensor")
    sites, places = lax.axis_size("site"), lax.axis_size("tensor")
    role = site % SITES
    hub = jnp.where(role == 3, (site + 1) % sites, site - role)
    channels, width = r_all.shape[3], r_all.shape[4]
    held = m_ref.shape[0]
    far = hub + 2
    end = (hub + sites - 1) % sites
    parity = jnp.where(role == 1, 1, 0)
    partner = hub + 1 - parity
    works = role < 2

    def at(step):
        return lax.rem(place + step + places, places)

    loads = [
        pltpu.make_async_copy(src, dst, load_sem.at[i])
        for i, (src, dst) in enumerate((
            (m_ref, raw), (size_in, size_ref), (live_in, live_ref),
            (mpo_in, mpo_ref), (mask_in, mask_ref),
        ))
    ]
    for load in loads:
        load.start()
    barrier = pltpu.get_barrier_semaphore()

    def greet(*targets):
        for site_to, place_to in targets:
            pl.semaphore_signal(barrier, inc=1, device_id=(site_to, place_to), device_id_type=MESH)

    @pl.when(works)
    def _():
        greet((far, place), (end, place), (partner, place), (site, at(1)), (site, at(-1)))

    @pl.when(role == 2)
    def _():
        greet((hub, place), (hub + 1, place), (site, at(1)), (site, at(-1)))

    @pl.when(role == 3)
    def _():
        greet((hub, place), (hub + 1, place))

    for load in loads[:3]:
        load.wait()
    for i in range(held):
        sector = place * held + i
        for s in range(PHYS):
            charge = CHARGE[s]
            live = (live_ref[0, i, charge] > 0) & (sector + charge < places * held)
            bound = jnp.where(live, size_ref[0, i], 0)
            block = jnp.where(ids(width, width, 0) < bound, raw[i, s].astype(F32), 0.0)
            ring[0, i, s] = block.astype(BF16)

    def load_weights():
        for load in loads[3:]:
            load.wait()

    def remote(src, dst, send, recv, site_to, place_to):
        return pltpu.make_async_remote_copy(
            src_ref=src, dst_ref=dst, send_sem=send, recv_sem=recv,
            device_id=(site_to, place_to), device_id_type=MESH,
        )

    def half(k, i, h):
        return ring.at[k, i, pl.ds(2 * h, 2)]

    def ring_copy(k, i, h):
        return remote(
            half(k, i, h), half(k + 1, i, h), ring_send.at[k, i, h], ring_recv.at[k + 1, i, h],
            site, at(-1),
        )

    def ring_wait(k, i, h):
        remote(
            half(k, i, h), half(k, i, h), ring_send.at[0, 0, 0], ring_recv.at[k, i, h],
            site, at(-1),
        ).wait_recv()

    def feed_half(k, i, h):
        return remote(
            half(k, i, h), m_all.at[0, k, pl.ds(2 * h, 2)], feed_send.at[k, i],
            feed_recv.at[0, k], hub + i, place,
        )

    def feed(turn, k, i, source, send):
        return remote(
            source, m_all.at[turn, k], send, feed_recv.at[turn, k], hub + i, place
        )

    def feed_wait(turn, k):
        part = m_all.at[turn, k]
        remote(
            part, part, pass_send.at[0, 0], feed_recv.at[turn, k], partner, place
        ).wait_recv()

    def pass_on(turn, k):
        return remote(
            m_all.at[turn, k], m_all.at[turn, k + 1], pass_send.at[turn, k],
            feed_recv.at[turn, k + 1], site, at(-1),
        )

    def pass_first(turn):
        return remote(
            ring.at[0, parity], m_all.at[turn, 1], pass_send.at[turn, 0],
            feed_recv.at[turn, 1], site, at(-1),
        )

    def start(blocks, target, slot):
        low = blocks[0]
        mid = blocks[1:3].reshape(2 * width, width)
        top = blocks[3]
        step = 32
        for row in range(0, width, step):
            g0 = nt(low[row : row + step], low)
            g1 = nt(mid[row : row + step], mid)
            g2 = nt(mid[width + row : width + row + step], mid)
            g3 = nt(top[row : row + step], top)
            parts = (g0, g1[:, :width], g1[:, width:], g2[:, :width], g2[:, width:], g3)
            parts = [x.reshape(step // 8, 8, width) for x in parts]
            for w in range(channels):
                block = parts[0] * coef[0, w][None]
                for i in range(1, len(PAIRS)):
                    block = block + parts[i] * coef[i, w][None]
                target[w, row : row + step, :] = block.reshape(step, width).astype(BF16)

        @pl.when(slot == 0)
        def _():
            small = target[...].astype(F32).reshape(channels * width // 8, 8, width) * SMALL
            squares[0, 0] += jnp.sum(small * small, axis=0)

    def swap_part(turn, j, part):
        last = turn == SITES - 1
        arrival = jnp.where(last, parity, j)
        return remote(
            part, part, swap_send.at[turn, j], swap_recv.at[turn, arrival],
            jnp.where(last, end, partner), place,
        )

    def swap(turn, j):
        return swap_part(turn, j, r_all.at[turn, parity, j])

    def swap_pair(turn, j, pair):
        @pl.when(swaps(turn, j))
        def _():
            swap_part(turn, j, r_all.at[turn, parity, j, pl.ds(2 * pair, 2)]).start()

    def advance(turn, j):
        prev = turn - 1
        low = m_all[turn, j, 0]
        mid = m_all[turn, j, 1:3].reshape(2 * width, width)
        top = m_all[turn, j, 3]
        step = 32

        one = channels * 8

        def keep(row, first, x):
            y = x.reshape(channels, step // 8, 8, width)
            for i in range(step // 16):
                cut = [y[:, 2 * i + h].reshape(one, width) for h in range(2)]
                both = jnp.concatenate(cut, axis=1).astype(BF16)
                inner[row // 16 + i, first : first + one] = both

        for row in range(0, width, step):
            def rows_of(which, slot):
                rows = r_all[prev, which, slot, :, row : row + step, :]
                return rows.reshape(channels * step, width)

            keep(row, 0, nt(rows_of(parity, j), low))
            x = nt(rows_of(1 - parity, j + parity), mid)
            keep(row, one, x[:, :width])
            keep(row, 2 * one, x[:, width:])
            keep(row, 3 * one, nt(rows_of(parity, j + 1), top))

        def put(s, i, y):
            z = y.reshape(channels, 8, 2 * width)
            at_row = s * width + 16 * i
            for w in range(channels):
                both = jnp.concatenate([z[w, :, :width], z[w, :, width:]], axis=0)
                lane = (w % 2) * width
                mixed[w // 2, at_row : at_row + 16, lane : lane + width] = both.astype(BF16)

        for i in range(width // 16):
            put(0, i, nn(mix_low[prev], inner[i, :one]))
        for i in range(width // 16):
            y = nn(mix_mid[prev], inner[i, one : 3 * one])
            put(1, i, y[:one])
            put(2, i, y[one:])
        for i in range(width // 16):
            put(3, i, nn(mix_top[prev], inner[i, 3 * one :]))
        wide = jnp.concatenate([low, mid[:width], mid[width:], top], axis=1)
        total = jnp.zeros((8, 2 * width), F32)
        for pair in range(channels // 2):
            block = nn(wide, mixed[pair])
            r_all[turn, parity, j, 2 * pair] = block[:, :width].astype(BF16)
            r_all[turn, parity, j, 2 * pair + 1] = block[:, width:].astype(BF16)
            small = block * SMALL
            total = total + jnp.sum((small * small).reshape(width // 8, 8, 2 * width), axis=0)
        slot = (j >= 1).astype(jnp.int32)
        squares[slot, turn] += total[:, :width] + total[:, width:]

        @pl.when(swaps(turn, j))
        def _():
            swap(turn, j).start()

    def swap_wait(turn, j):
        part = r_all.at[turn, 1 - parity, j]
        remote(
            part, part, swap_send.at[turn, j], swap_recv.at[turn, j], partner, place
        ).wait_recv()

    def swaps(turn, j):
        even = (parity == 0) & ((j >= 1) | (turn == 1))
        odd = (parity == 1) & (j <= 2 - turn)
        return (turn == 3) | even | odd

    def tell(i):
        for step in (ROUNDS[i], -ROUNDS[i]):
            pl.semaphore_signal(
                round_sem.at[i], inc=1, device_id=(site, at(step)), device_id_type=MESH
            )

    def told(i):
        pl.semaphore_wait(round_sem.at[i], 2)

    targets = (end, hub, hub + 1, far)

    def sum_copy(kind, step):
        return remote(
            mine, heard.at[parity * places + place], sum_send.at[kind, step], sum_recv,
            targets[kind], at(step),
        )

    def sum_self(kind, step):
        return (step == 0) & (kind == parity + 1)

    @pl.when(role == 2)
    def _():
        pl.semaphore_wait(barrier, 4)

        @pl.loop(0, REACH)
        def _(k):
            for i in range(held):
                for h in range(2):
                    @pl.when(k > 0)
                    def _():
                        ring_wait(k, i, h)

                    @pl.when(k < REACH - 1)
                    def _():
                        ring_copy(k, i, h).start()

                    feed_half(k, i, h).start()

        load_weights()
        edge_of(table_of(SITES - 1, mpo_ref, mask_ref, table), channels, coef)
        squares[...] = jnp.zeros_like(squares)

        @pl.loop(0, held)
        def _(i):
            start(ring.at[0, i], r_all.at[0, i, 0], 1)

    @pl.when(role == 3)
    def _():
        pl.semaphore_wait(barrier, 2)
        for i in range(held):
            feed(3, 0, i, ring.at[0, i], feed_send.at[0, i]).start()
        load_weights()

    @pl.when(works)
    def _():
        home = 2 - parity
        pl.semaphore_wait(barrier, 5)
        tell(0)
        feed(home, 0, 1 - parity, ring.at[0, 1 - parity], feed_send.at[0, 0]).start()
        pass_first(home).start()
        m_all[home, 0] = ring[0, parity]
        load_weights()
        edge_of(table_of(SITES - 1, mpo_ref, mask_ref, table), channels, coef)
        squares[...] = jnp.zeros_like(squares)
        feed_wait(1 + parity, 0)
        pass_on(1 + parity, 0).start()
        told(0)
        tell(1)
        for turn in range(1, SITES):
            found = table_of(SITES - 1 - turn, mpo_ref, mask_ref, table)
            mix_low[turn - 1] = spread(found, channels, 0, 1)
            mix_mid[turn - 1] = spread(found, channels, 1, 2)
            mix_top[turn - 1] = spread(found, channels, 3, 1)

        @pl.loop(0, REACH)
        def _(k):
            feed_wait(0, k)
            start(m_all.at[0, k], r_all.at[0, parity, k], (k >= 1).astype(jnp.int32))

            @pl.when(swaps(0, k))
            def _():
                swap(0, k).start()

            @pl.loop(1, k + 1)
            def _(t):
                @pl.when(k == REACH - 1)
                def _():
                    feed_wait(t, k - t)

                swap_wait(t - 1, k - t + parity)
                advance(t, k - t)

            @pl.when(k == 0)
            def _():
                feed_wait(1, 1)
                pass_on(1, 1).start()
                told(1)
                tell(2)

            @pl.when(k == 1)
            def _():
                told(2)
                tell(3)

        lane = ids(1, width, 1)
        row = jnp.zeros((1, width), F32)
        for t in range(SITES):
            row = row + jnp.where(lane == t, jnp.sum(squares[0, t]), 0.0)
        mine[...] = row
        heard[parity * places + place] = row
        told(3)

        for kind in range(4):
            @pl.loop(0, places)
            def _(step):
                @pl.when(jnp.logical_not(sum_self(kind, step)))
                def _():
                    sum_copy(kind, step).start()

    @pl.when(works)
    def _():
        home = 2 - parity
        feed(home, 0, 1 - parity, ring.at[0, 1 - parity], feed_send.at[0, 0]).wait_send()
        for t, k in ((1, 0), (1, 1), (2, 0)):
            pass_on(t, k).wait_send()
        for t in range(SITES):
            for j in range(REACH - t):
                @pl.when(swaps(t, j))
                def _():
                    swap(t, j).wait_send()
        for kind in range(4):
            @pl.loop(0, places)
            def _(step):
                @pl.when(jnp.logical_not(sum_self(kind, step)))
                def _():
                    sum_copy(kind, step).wait_send()

    @pl.when(role == 2)
    def _():
        for k in range(REACH):
            for i in range(held):
                for h in range(2):
                    if k < REACH - 1:
                        ring_copy(k, i, h).wait_send()
                feed(0, k, i, ring.at[k, i], feed_send.at[k, i]).wait_send()

    @pl.when(role == 3)
    def _():
        for i in range(held):
            feed(3, 0, i, ring.at[0, i], feed_send.at[0, i]).wait_send()

    def heard_all(count):
        part = heard.at[pl.ds(0, count)]
        remote(part, part, sum_send.at[0, 0], sum_recv, site, at(1)).wait_recv()

    @pl.when(role == 3)
    def _():
        for i in range(held):
            part = r_all.at[3, i, 0]
            remote(
                part, part, swap_send.at[3, 0], swap_recv.at[3, i], hub + i, place
            ).wait_recv()

    @pl.when(role == 1)
    def _():
        swap_wait(1, 0)

    turn = jnp.where(role == 3, 3, 2 - role)
    for i in range(held):
        out_ref[i] = r_all[turn, i, 0]

    @pl.when(works)
    def _():
        heard_all(2 * places - 1)

    @pl.when(role >= 2)
    def _():
        heard_all(2 * places)

    sums = jnp.sum(heard[...].reshape(2 * places, width), axis=0, keepdims=True)
    entries = float(places * held * channels * width * width)
    unit = jnp.ones((1, 1), F32)
    chosen = unit
    for t in range(SITES):
        square = sums[:, t : t + 1] * (1.0 / (SMALL * SMALL * entries)) * unit * unit
        unit = unit * lax.rsqrt(square + EPSILON)
        chosen = jnp.where(turn == t, unit, chosen)
    scale_ref[...] = jnp.broadcast_to(chosen, scale_ref.shape)


def scaled(in_ref, scale_ref, out_ref, final, done_sem):
    channels = final.shape[1]
    factor = scale_ref[0:1, :].reshape(1, 1, final.shape[-1])

    def put(w):
        return pltpu.make_async_copy(final.at[:, w], out_ref.at[:, w], done_sem.at[w])

    for w in range(channels):
        final[:, w] = (in_ref[:, w].astype(F32) * factor).astype(BF16)
        put(w).start()
    for w in range(channels):
        put(w).wait()


def on_device(mps, mpo, mpo_mask, sector_size, pair_live):
    places = lax.axis_size("tensor")
    held, width = mps.shape[1], mps.shape[-1]
    channels = mpo.shape[1]
    vmem, dma = pltpu.VMEM, pltpu.SemaphoreType.DMA
    in_vmem, in_hbm = pl.BlockSpec(memory_space=pltpu.VMEM), pl.BlockSpec(memory_space=pltpu.HBM)
    result = (held, channels, width, width)
    environment, scale = pl.pallas_call(
        kernel,
        out_shape=(
            jax.ShapeDtypeStruct(result, BF16),
            jax.ShapeDtypeStruct((8, width), F32),
        ),
        in_specs=[in_hbm] * 5,
        out_specs=(in_vmem, in_vmem),
        scratch_shapes=[
            vmem((SITES, channels, PHYS, PHYS, channels), BF16),
            vmem((channels, SITES, channels), jnp.int32),
            pltpu.SMEM((1, held), jnp.int32),
            pltpu.SMEM((1, held, 3), jnp.int32),
            vmem((held, PHYS, width, width), BF16),
            vmem((REACH, held, PHYS, width, width), BF16),
            vmem((SITES, REACH, PHYS, width, width), BF16),
            vmem((SITES, 2, REACH, channels, width, width), BF16),
            vmem((SITES - 1, channels * 8, channels * 8), BF16),
            vmem((SITES - 1, channels * 16, channels * 16), BF16),
            vmem((SITES - 1, channels * 8, channels * 8), BF16),
            vmem((len(PAIRS), channels, 8, width), F32),
            vmem((channels * PHYS * PHYS, width), F32),
            vmem((width // 16, PHYS * channels * 8, 2 * width), BF16),
            vmem((channels // 2, PHYS * width, 2 * width), BF16),
            vmem((2, SITES, 8, width), F32),
            vmem((1, width), F32),
            vmem((2 * places, 1, width), F32),
            dma((5,)),
            dma((REACH, held, 2)),
            dma((REACH, held, 2)),
            dma((REACH, held)),
            dma((SITES, REACH)),
            dma((SITES, REACH)),
            dma((SITES, REACH)),
            dma((SITES, REACH)),
            dma((SITES, places)),
            dma,
            pltpu.SemaphoreType.REGULAR((len(ROUNDS),)),
        ],
        compiler_params=pltpu.CompilerParams(
            collective_id=0, has_side_effects=True, vmem_limit_bytes=48 * 1024 * 1024
        ),
    )(
        *[
            pltpu.with_memory_space_constraint(x, pltpu.HBM)
            for x in (
                mps[0],
                jnp.transpose(mpo, (0, 1, 3, 4, 2)),
                jnp.transpose(mpo_mask, (1, 0, 2)),
                sector_size,
                pair_live,
            )
        ]
    )
    return pl.pallas_call(
        scaled,
        out_shape=jax.ShapeDtypeStruct(result, BF16),
        in_specs=[in_vmem, in_vmem],
        out_specs=pl.BlockSpec(memory_space=pl.ANY),
        scratch_shapes=[vmem(result, BF16), dma((channels,))],
        compiler_params=pltpu.CompilerParams(vmem_limit_bytes=4 * 1024 * 1024),
    )(environment, scale)[None]


def solution(mesh):
    in_specs = (
        P("site", "tensor", None, None, None),
        P(),
        P(),
        P("site", "tensor"),
        P("site", "tensor", None),
    )
    out_specs = P("site", "tensor", None, None, None)
    return jax.shard_map(
        on_device, mesh=mesh, in_specs=in_specs, out_specs=out_specs, check_vma=False
    )
```

```python
import jax
import jax.numpy as jnp
from jax import lax
from jax.experimental import pallas as pl
from jax.experimental.pallas import tpu as pltpu
from jax.sharding import PartitionSpec as P

SITES = 4
PHYS = 4
CHARGE = (0, 1, 1, 2)
PAIRS = (0, 5, 6, 9, 10, 15)
ROUNDS = (1, 2, 4, 1)
MESH = pl.DeviceIdType.MESH
EPSILON = 1e-06
SMALL = 2.0**-12
F32 = jnp.float32
BF16 = jnp.bfloat16
REACH = 4


def nt(a, b):
    return lax.dot_general(a, b, (((1,), (1,)), ((), ())), preferred_element_type=F32)


def nn(a, b):
    return lax.dot_general(a, b, (((1,), (0,)), ((), ())), preferred_element_type=F32)


def ids(rows, columns, axis):
    return lax.broadcasted_iota(jnp.int32, (rows, columns), axis)


def table_of(p, mpo_ref, mask_ref, table):
    channels = mask_ref.shape[0]
    table[...] = jnp.zeros_like(table)
    for w in range(channels):
        keep = mask_ref[w, p : p + 1, :] > 0
        for s in range(PHYS):
            tile = jnp.where(keep, mpo_ref[p, w, s].astype(F32), 0.0)
            at = (w * PHYS + s) * PHYS
            table[at : at + PHYS, :channels] = tile
    return table[...].astype(BF16)


def one_hot(condition):
    return jnp.where(condition, 1.0, 0.0).astype(BF16)


def spread(table, channels, first, count):
    one = channels * 8
    size, depth = count * one, table.shape[0]

    def split(x):
        state = jnp.where(x >= one, 1, 0)
        return state + first, (x - state * one) // 8

    _, channel_of_column = split(ids(table.shape[1], size, 1))
    wide = nn(table, one_hot(ids(table.shape[1], size, 0) == channel_of_column))
    state_of_column, _ = split(ids(depth, size, 1))
    wide = jnp.where(ids(depth, size, 0) % PHYS == state_of_column, wide, 0.0).astype(BF16)
    state_of_row, channel_of_row = split(ids(size, depth, 0))
    entry = ids(size, depth, 1)
    pick = one_hot(entry // PHYS == channel_of_row * PHYS + state_of_row)
    full = nn(pick, wide)
    return jnp.where(ids(size, size, 0) % 8 == ids(size, size, 1) % 8, full, 0.0).astype(BF16)


def edge_of(table, channels, coef):
    depth, lanes = table.shape
    last = nn(table, one_hot(ids(lanes, lanes, 0) == channels - 1)).astype(BF16)
    rows = channels * 8
    for i, code in enumerate(PAIRS):
        pick = one_hot(ids(rows, depth, 1) == ids(rows, depth, 0) // 8 * PHYS * PHYS + code)
        coef[i] = nn(pick, last).reshape(channels, 8, lanes)


def kernel(
    m_ref, mpo_in, mask_in, size_in, live_in, out_ref, scale_ref,
    mpo_ref, mask_ref, size_ref, live_ref, raw, ring, m_all, r_all, mix_low, mix_mid, mix_top, coef, table, inner, mixed, squares, mine, heard,
    load_sem, ring_send, ring_recv, feed_send, feed_recv, pass_send, swap_send, swap_recv,
    sum_send, sum_recv, round_sem,
):
    site, place = lax.axis_index("site"), lax.axis_index("tensor")
    sites, places = lax.axis_size("site"), lax.axis_size("tensor")
    role = site % SITES
    hub = jnp.where(role == 3, (site + 1) % sites, site - role)
    channels, width = r_all.shape[3], r_all.shape[4]
    held = m_ref.shape[0]
    far = hub + 2
    end = (hub + sites - 1) % sites
    parity = jnp.where(role == 1, 1, 0)
    partner = hub + 1 - parity
    works = role < 2

    def at(step):
        return lax.rem(place + step + places, places)

    loads = [
        pltpu.make_async_copy(src, dst, load_sem.at[i])
        for i, (src, dst) in enumerate((
            (m_ref, raw), (size_in, size_ref), (live_in, live_ref),
            (mpo_in, mpo_ref), (mask_in, mask_ref),
        ))
    ]
    for load in loads:
        load.start()
    barrier = pltpu.get_barrier_semaphore()

    def greet(*targets):
        for site_to, place_to in targets:
            pl.semaphore_signal(barrier, inc=1, device_id=(site_to, place_to), device_id_type=MESH)

    @pl.when(works)
    def _():
        greet((far, place), (end, place), (partner, place), (site, at(1)), (site, at(-1)))

    @pl.when(role == 2)
    def _():
        greet((hub, place), (hub + 1, place), (site, at(1)), (site, at(-1)))

    @pl.when(role == 3)
    def _():
        greet((hub, place), (hub + 1, place))

    for load in loads[:3]:
        load.wait()
    for i in range(held):
        sector = place * held + i
        for s in range(PHYS):
            charge = CHARGE[s]
            live = (live_ref[0, i, charge] > 0) & (sector + charge < places * held)
            bound = jnp.where(live, size_ref[0, i], 0)
            block = jnp.where(ids(width, width, 0) < bound, raw[i, s].astype(F32), 0.0)
            ring[0, i, s] = block.astype(BF16)

    def load_weights():
        for load in loads[3:]:
            load.wait()

    def remote(src, dst, send, recv, site_to, place_to):
        return pltpu.make_async_remote_copy(
            src_ref=src, dst_ref=dst, send_sem=send, recv_sem=recv,
            device_id=(site_to, place_to), device_id_type=MESH,
        )

    def half(k, i, h):
        return ring.at[k, i, pl.ds(2 * h, 2)]

    def ring_copy(k, i, h):
        return remote(
            half(k, i, h), half(k + 1, i, h), ring_send.at[k, i, h], ring_recv.at[k + 1, i, h],
            site, at(-1),
        )

    def ring_wait(k, i, h):
        remote(
            half(k, i, h), half(k, i, h), ring_send.at[0, 0, 0], ring_recv.at[k, i, h],
            site, at(-1),
        ).wait_recv()

    def feed_half(k, i, h):
        return remote(
            half(k, i, h), m_all.at[0, k, pl.ds(2 * h, 2)], feed_send.at[k, i],
            feed_recv.at[0, k], hub + i, place,
        )

    def feed(turn, k, i, source, send):
        return remote(
            source, m_all.at[turn, k], send, feed_recv.at[turn, k], hub + i, place
        )

    def feed_wait(turn, k):
        part = m_all.at[turn, k]
        remote(
            part, part, pass_send.at[0, 0], feed_recv.at[turn, k], partner, place
        ).wait_recv()

    def pass_on(turn, k):
        return remote(
            m_all.at[turn, k], m_all.at[turn, k + 1], pass_send.at[turn, k],
            feed_recv.at[turn, k + 1], site, at(-1),
        )

    def pass_first(turn):
        return remote(
            ring.at[0, parity], m_all.at[turn, 1], pass_send.at[turn, 0],
            feed_recv.at[turn, 1], site, at(-1),
        )

    def start(blocks, target, slot):
        low = blocks[0]
        mid = blocks[1:3].reshape(2 * width, width)
        top = blocks[3]
        step = 32
        for row in range(0, width, step):
            g0 = nt(low[row : row + step], low)
            g1 = nt(mid[row : row + step], mid)
            g2 = nt(mid[width + row : width + row + step], mid)
            g3 = nt(top[row : row + step], top)
            parts = (g0, g1[:, :width], g1[:, width:], g2[:, :width], g2[:, width:], g3)
            parts = [x.reshape(step // 8, 8, width) for x in parts]
            for w in range(channels):
                block = parts[0] * coef[0, w][None]
                for i in range(1, len(PAIRS)):
                    block = block + parts[i] * coef[i, w][None]
                target[w, row : row + step, :] = block.reshape(step, width).astype(BF16)

        @pl.when(slot == 0)
        def _():
            small = target[...].astype(F32).reshape(channels * width // 8, 8, width) * SMALL
            squares[0, 0] += jnp.sum(small * small, axis=0)

    def swap_part(turn, j, part):
        last = turn == SITES - 1
        arrival = jnp.where(last, parity, j)
        return remote(
            part, part, swap_send.at[turn, j], swap_recv.at[turn, arrival],
            jnp.where(last, end, partner), place,
        )

    def swap(turn, j):
        return swap_part(turn, j, r_all.at[turn, parity, j])

    def swap_pair(turn, j, pair):
        @pl.when(swaps(turn, j))
        def _():
            swap_part(turn, j, r_all.at[turn, parity, j, pl.ds(2 * pair, 2)]).start()

    def advance(turn, j):
        prev = turn - 1
        low = m_all[turn, j, 0]
        mid = m_all[turn, j, 1:3].reshape(2 * width, width)
        top = m_all[turn, j, 3]
        step = 32

        one = channels * 8

        def keep(row, first, x):
            y = x.reshape(channels, step // 8, 8, width)
            for i in range(step // 16):
                cut = [y[:, 2 * i + h].reshape(one, width) for h in range(2)]
                both = jnp.concatenate(cut, axis=1).astype(BF16)
                inner[row // 16 + i, first : first + one] = both

        for row in range(0, width, step):
            def rows_of(which, slot):
                rows = r_all[prev, which, slot, :, row : row + step, :]
                return rows.reshape(channels * step, width)

            keep(row, 0, nt(rows_of(parity, j), low))
            x = nt(rows_of(1 - parity, j + parity), mid)
            keep(row, one, x[:, :width])
            keep(row, 2 * one, x[:, width:])
            keep(row, 3 * one, nt(rows_of(parity, j + 1), top))

        def put(s, i, y):
            z = y.reshape(channels, 8, 2 * width)
            at_row = s * width + 16 * i
            for w in range(channels):
                both = jnp.concatenate([z[w, :, :width], z[w, :, width:]], axis=0)
                lane = (w % 2) * width
                mixed[w // 2, at_row : at_row + 16, lane : lane + width] = both.astype(BF16)

        for i in range(width // 16):
            put(0, i, nn(mix_low[prev], inner[i, :one]))
        for i in range(width // 16):
            y = nn(mix_mid[prev], inner[i, one : 3 * one])
            put(1, i, y[:one])
            put(2, i, y[one:])
        for i in range(width // 16):
            put(3, i, nn(mix_top[prev], inner[i, 3 * one :]))
        wide = jnp.concatenate([low, mid[:width], mid[width:], top], axis=1)
        total = jnp.zeros((8, 2 * width), F32)
        for pair in range(channels // 2):
            block = nn(wide, mixed[pair])
            r_all[turn, parity, j, 2 * pair] = block[:, :width].astype(BF16)
            r_all[turn, parity, j, 2 * pair + 1] = block[:, width:].astype(BF16)
            small = block * SMALL
            total = total + jnp.sum((small * small).reshape(width // 8, 8, 2 * width), axis=0)

        @pl.when(swaps(turn, j))
        def _():
            swap(turn, j).start()

        slot = (j >= 1).astype(jnp.int32)
        squares[slot, turn] += total[:, :width] + total[:, width:]

    def swap_wait(turn, j):
        part = r_all.at[turn, 1 - parity, j]
        remote(
            part, part, swap_send.at[turn, j], swap_recv.at[turn, j], partner, place
        ).wait_recv()

    def swaps(turn, j):
        even = (parity == 0) & ((j >= 1) | (turn == 1))
        odd = (parity == 1) & (j <= 2 - turn)
        return (turn == 3) | even | odd

    def tell(i):
        for step in (ROUNDS[i], -ROUNDS[i]):
            pl.semaphore_signal(
                round_sem.at[i], inc=1, device_id=(site, at(step)), device_id_type=MESH
            )

    def told(i):
        pl.semaphore_wait(round_sem.at[i], 2)

    targets = (end, hub, hub + 1, far)

    def sum_copy(kind, step):
        return remote(
            mine, heard.at[parity * places + place], sum_send.at[kind, step], sum_recv,
            targets[kind], at(step),
        )

    def sum_self(kind, step):
        return (step == 0) & (kind == parity + 1)

    @pl.when(role == 2)
    def _():
        pl.semaphore_wait(barrier, 4)

        @pl.loop(0, REACH)
        def _(k):
            for i in range(held):
                for h in range(2):
                    @pl.when(k > 0)
                    def _():
                        ring_wait(k, i, h)

                    @pl.when(k < REACH - 1)
                    def _():
                        ring_copy(k, i, h).start()

                    feed_half(k, i, h).start()

        load_weights()
        edge_of(table_of(SITES - 1, mpo_ref, mask_ref, table), channels, coef)
        squares[...] = jnp.zeros_like(squares)

        @pl.loop(0, held)
        def _(i):
            start(ring.at[0, i], r_all.at[0, i, 0], 1)

    @pl.when(role == 3)
    def _():
        pl.semaphore_wait(barrier, 2)
        for i in range(held):
            feed(3, 0, i, ring.at[0, i], feed_send.at[0, i]).start()
        load_weights()

    @pl.when(works)
    def _():
        home = 2 - parity
        pl.semaphore_wait(barrier, 5)
        tell(0)
        feed(home, 0, 1 - parity, ring.at[0, 1 - parity], feed_send.at[0, 0]).start()
        pass_first(home).start()
        m_all[home, 0] = ring[0, parity]
        load_weights()
        edge_of(table_of(SITES - 1, mpo_ref, mask_ref, table), channels, coef)
        squares[...] = jnp.zeros_like(squares)
        feed_wait(1 + parity, 0)
        pass_on(1 + parity, 0).start()
        told(0)
        tell(1)
        for turn in range(1, SITES):
            found = table_of(SITES - 1 - turn, mpo_ref, mask_ref, table)
            mix_low[turn - 1] = spread(found, channels, 0, 1)
            mix_mid[turn - 1] = spread(found, channels, 1, 2)
            mix_top[turn - 1] = spread(found, channels, 3, 1)

        @pl.loop(0, REACH)
        def _(k):
            feed_wait(0, k)
            start(m_all.at[0, k], r_all.at[0, parity, k], (k >= 1).astype(jnp.int32))

            @pl.when(swaps(0, k))
            def _():
                swap(0, k).start()

            @pl.loop(1, k + 1)
            def _(t):
                @pl.when(k == REACH - 1)
                def _():
                    feed_wait(t, k - t)

                swap_wait(t - 1, k - t + parity)
                advance(t, k - t)

            @pl.when(k == 0)
            def _():
                feed_wait(1, 1)
                pass_on(1, 1).start()
                told(1)
                tell(2)

            @pl.when(k == 1)
            def _():
                told(2)
                tell(3)

        lane = ids(1, width, 1)
        row = jnp.zeros((1, width), F32)
        for t in range(SITES):
            row = row + jnp.where(lane == t, jnp.sum(squares[0, t]), 0.0)
        mine[...] = row
        heard[parity * places + place] = row
        told(3)

        @pl.loop(0, places)
        def _(step):
            sum_copy(0, step).start()

        for kind in range(1, 4):
            @pl.loop(0, places)
            def _(step):
                @pl.when(jnp.logical_not(sum_self(kind, step)))
                def _():
                    sum_copy(kind, step).start()

    @pl.when(works)
    def _():
        home = 2 - parity
        feed(home, 0, 1 - parity, ring.at[0, 1 - parity], feed_send.at[0, 0]).wait_send()
        for t, k in ((1, 0), (1, 1), (2, 0)):
            pass_on(t, k).wait_send()
        for t in range(SITES):
            for j in range(REACH - t):
                @pl.when(swaps(t, j))
                def _():
                    swap(t, j).wait_send()
        for kind in range(4):
            @pl.loop(0, places)
            def _(step):
                @pl.when(jnp.logical_not(sum_self(kind, step)))
                def _():
                    sum_copy(kind, step).wait_send()

    @pl.when(role == 2)
    def _():
        for k in range(REACH):
            for i in range(held):
                for h in range(2):
                    if k < REACH - 1:
                        ring_copy(k, i, h).wait_send()
                feed(0, k, i, ring.at[k, i], feed_send.at[k, i]).wait_send()

    @pl.when(role == 3)
    def _():
        for i in range(held):
            feed(3, 0, i, ring.at[0, i], feed_send.at[0, i]).wait_send()

    def heard_all(count):
        part = heard.at[pl.ds(0, count)]
        remote(part, part, sum_send.at[0, 0], sum_recv, site, at(1)).wait_recv()

    @pl.when(role == 3)
    def _():
        for i in range(held):
            part = r_all.at[3, i, 0]
            remote(
                part, part, swap_send.at[3, 0], swap_recv.at[3, i], hub + i, place
            ).wait_recv()

    @pl.when(role == 1)
    def _():
        swap_wait(1, 0)

    turn = jnp.where(role == 3, 3, 2 - role)
    for i in range(held):
        out_ref[i] = r_all[turn, i, 0]

    @pl.when(works)
    def _():
        heard_all(2 * places - 1)

    @pl.when(role >= 2)
    def _():
        heard_all(2 * places)

    sums = jnp.sum(heard[...].reshape(2 * places, width), axis=0, keepdims=True)
    entries = float(places * held * channels * width * width)
    unit = jnp.ones((1, 1), F32)
    chosen = unit
    for t in range(SITES):
        square = sums[:, t : t + 1] * (1.0 / (SMALL * SMALL * entries)) * unit * unit
        unit = unit * lax.rsqrt(square + EPSILON)
        chosen = jnp.where(turn == t, unit, chosen)
    scale_ref[...] = jnp.broadcast_to(chosen, scale_ref.shape)


def scaled(in_ref, scale_ref, out_ref, final, done_sem):
    channels = final.shape[1]
    factor = scale_ref[0:1, :].reshape(1, 1, final.shape[-1])

    def put(w):
        return pltpu.make_async_copy(final.at[:, w], out_ref.at[:, w], done_sem.at[w])

    for w in range(channels):
        final[:, w] = (in_ref[:, w].astype(F32) * factor).astype(BF16)
        put(w).start()
    for w in range(channels):
        put(w).wait()


def on_device(mps, mpo, mpo_mask, sector_size, pair_live):
    places = lax.axis_size("tensor")
    held, width = mps.shape[1], mps.shape[-1]
    channels = mpo.shape[1]
    vmem, dma = pltpu.VMEM, pltpu.SemaphoreType.DMA
    in_vmem, in_hbm = pl.BlockSpec(memory_space=pltpu.VMEM), pl.BlockSpec(memory_space=pltpu.HBM)
    result = (held, channels, width, width)
    environment, scale = pl.pallas_call(
        kernel,
        out_shape=(
            jax.ShapeDtypeStruct(result, BF16),
            jax.ShapeDtypeStruct((8, width), F32),
        ),
        in_specs=[in_hbm] * 5,
        out_specs=(in_vmem, in_vmem),
        scratch_shapes=[
            vmem((SITES, channels, PHYS, PHYS, channels), BF16),
            vmem((channels, SITES, channels), jnp.int32),
            pltpu.SMEM((1, held), jnp.int32),
            pltpu.SMEM((1, held, 3), jnp.int32),
            vmem((held, PHYS, width, width), BF16),
            vmem((REACH, held, PHYS, width, width), BF16),
            vmem((SITES, REACH, PHYS, width, width), BF16),
            vmem((SITES, 2, REACH, channels, width, width), BF16),
            vmem((SITES - 1, channels * 8, channels * 8), BF16),
            vmem((SITES - 1, channels * 16, channels * 16), BF16),
            vmem((SITES - 1, channels * 8, channels * 8), BF16),
            vmem((len(PAIRS), channels, 8, width), F32),
            vmem((channels * PHYS * PHYS, width), F32),
            vmem((width // 16, PHYS * channels * 8, 2 * width), BF16),
            vmem((channels // 2, PHYS * width, 2 * width), BF16),
            vmem((2, SITES, 8, width), F32),
            vmem((1, width), F32),
            vmem((2 * places, 1, width), F32),
            dma((5,)),
            dma((REACH, held, 2)),
            dma((REACH, held, 2)),
            dma((REACH, held)),
            dma((SITES, REACH)),
            dma((SITES, REACH)),
            dma((SITES, REACH)),
            dma((SITES, REACH)),
            dma((SITES, places)),
            dma,
            pltpu.SemaphoreType.REGULAR((len(ROUNDS),)),
        ],
        compiler_params=pltpu.CompilerParams(
            collective_id=0, has_side_effects=True, vmem_limit_bytes=48 * 1024 * 1024
        ),
    )(
        *[
            pltpu.with_memory_space_constraint(x, pltpu.HBM)
            for x in (
                mps[0],
                jnp.transpose(mpo, (0, 1, 3, 4, 2)),
                jnp.transpose(mpo_mask, (1, 0, 2)),
                sector_size,
                pair_live,
            )
        ]
    )
    return pl.pallas_call(
        scaled,
        out_shape=jax.ShapeDtypeStruct(result, BF16),
        in_specs=[in_vmem, in_vmem],
        out_specs=pl.BlockSpec(memory_space=pl.ANY),
        scratch_shapes=[vmem(result, BF16), dma((channels,))],
        compiler_params=pltpu.CompilerParams(vmem_limit_bytes=4 * 1024 * 1024),
    )(environment, scale)[None]


def solution(mesh):
    in_specs = (
        P("site", "tensor", None, None, None),
        P(),
        P(),
        P("site", "tensor"),
        P("site", "tensor", None),
    )
    out_specs = P("site", "tensor", None, None, None)
    return jax.shard_map(
        on_device, mesh=mesh, in_specs=in_specs, out_specs=out_specs, check_vma=False
    )
```
